256 devices in a mesh: src: 4 (over y), tgt: 64 (over x, z, core).
Axes of the slice: x: 4, y: 4, z: 8, core: 2. Of those that a mesh axis runs over, the one named last changes fastest.
Arguments:
- source_cells: bfloat16 [32768, 256], P(('src', 'tgt')), may hold values from -16 to 16
- target_cells: bfloat16 [65536, 256], P('tgt'), may hold values from -6 to 6
- mapping: bfloat16 [256, 256], replicated, may hold values from -2 to 2
- source_logmass: bfloat16 [32768], P(('src', 'tgt')), may hold values from -1 to 1
- target_logmass: bfloat16 [65536], P('tgt'), may hold values from -1 to 1
- group_blocks: int32 [4], replicated, may hold values from 16 to 64, as said below
- tile_source: int32 [256, 64], P(('src', 'tgt')), may hold values from -1 to 63, as said below
- tile_target: int32 [256, 64], P(('src', 'tgt')), may hold values from -1 to 7, as said below
Outputs:
- source_potential: float32 [32768], P(('src', 'tgt'))
- target_potential: float32 [65536], P('tgt')
- map_gradient: float32 [256, 256], replicated
The draws below stay inside these ranges and needn't reach their ends.
Inputs may be any that keep to these rules, and one draw needn't show every extreme that they name: `group_blocks`: one group has all 64 blocks live. `tile_source`: -1 marks an empty slot and empty slots follow the used ones. Only live source blocks appear. No (source block, target block) pair appears twice in a group. Every live source block of a group appears on some device of that group, every target block of a device appears in its used slots, and some device uses all 64 slots. `tile_target`: -1 exactly where tile_source is -1.
All inputs are finite; a program needn't handle non-finite values.
Results may differ from the reference program's by a relative error of at most 0.0003.
The reference program's roundings to bfloat16 on the way (of `mapped` and `weights`) count: a program that leaves them out, or rounds other values in their place, can miss the bound.
Values may be sent and summed in bfloat16 or wider, within the bound.
No kernel may reach another device: no remote copies, remote signals or barrier semaphores. Data moves between devices by JAX's collectives and lax.ppermute only.
A program may use at most 128 MiB of HBM per device.

```python
import math
import jax
import jax.numpy as jnp
from jax import lax

D = 256
TILE = 128
TB_DEV = 8
TILES = 64
SINK = 4
ADJ = 4
GRP_CELLS = 8192
NS = 32768
NT = 65536
N_SRC = 4
N_TGT = 64


def tile_plan(key):
    plan_key = jax.random.fold_in(key, 11)
    key_busiest, key_blocks, key_offset, key_shift = jax.random.split(plan_key, 4)
    busiest = jax.random.randint(key_busiest, (), 0, N_SRC)
    blocks = jax.random.randint(key_blocks, (N_SRC,), max(N_TGT // 4, 1), N_TGT + 1)
    blocks = jnp.where(jnp.arange(N_SRC) == busiest, N_TGT, blocks).astype(jnp.int32)
    counts = jnp.maximum(TB_DEV, TILES * blocks // N_TGT)
    period = blocks * TB_DEV
    offsets = jax.random.randint(key_offset, (N_SRC,), 0, N_TGT * TB_DEV)
    shifts = jax.random.randint(key_shift, (N_SRC, N_TGT), 0, TB_DEV)
    column_index = jnp.arange(N_TGT)[None, :, None]
    slot_index = jnp.arange(TILES)[None, None, :]
    position = (column_index * counts[:, None, None] + slot_index + offsets[:, None, None]) % period[:, None, None]
    source_block = position // TB_DEV
    target_block = (position + shifts[:, :, None]) % TB_DEV
    used_slot = slot_index < counts[:, None, None]
    source_block = jnp.where(used_slot, source_block, -1).reshape(N_SRC * N_TGT, TILES).astype(jnp.int32)
    target_block = jnp.where(used_slot, target_block, -1).reshape(N_SRC * N_TGT, TILES).astype(jnp.int32)
    return (blocks, source_block, target_block)


def cell_values(key):
    blocks, source_block, target_block = tile_plan(key)
    key_target = jax.random.fold_in(key, 21)
    key_source = jax.random.fold_in(key, 22)
    key_sign = jax.random.fold_in(key, 23)
    targets = jnp.clip(jax.random.normal(key_target, (NT, D), jnp.float32), -6.0, 6.0)
    sources = jnp.clip(jax.random.normal(key_source, (NS, D), jnp.float32), -6.0, 6.0)
    group_rows = jnp.arange(N_SRC) * N_TGT
    picked_source = source_block[group_rows, 0]
    picked_target = target_block[group_rows, 0]
    source_rows = jnp.arange(N_SRC) * GRP_CELLS + picked_source * TILE
    target_rows = picked_target * TILE
    signs = jnp.where(jax.random.bernoulli(key_sign, 0.5, (N_SRC, D)), 1.0, -1.0).astype(jnp.float32)
    strength = 5.0 + 3.0 * jnp.arange(N_SRC, dtype=jnp.float32)
    changed = jnp.ceil(16.0 * math.sqrt(D) / strength)
    lowered = jnp.where(jnp.arange(D, dtype=jnp.float32)[None, :] < changed[:, None], 1.9375, 2.0)
    targets = targets.at[target_rows].set(2.0 * signs)
    targets = targets.at[target_rows + 1].set(lowered * signs)
    sources = sources.at[source_rows].set(strength[:, None] * signs)
    return (sources, targets)


def draw_source_cells(key, part):
    return cell_values(key)[0].astype(jnp.bfloat16)


def draw_target_cells(key, part):
    return cell_values(key)[1].astype(jnp.bfloat16)


def draw_mapping(key, part):
    noise_key = jax.random.fold_in(key, 31)
    noise = jnp.clip(jax.random.normal(noise_key, (D, D), jnp.float32), -6.0, 6.0)
    return (jnp.eye(D, dtype=jnp.float32) + noise * (0.5 / math.sqrt(D))).astype(jnp.bfloat16)


def draw_group_blocks(key, part):
    return tile_plan(key)[0]


def draw_tile_source(key, part):
    return tile_plan(key)[1]


def draw_tile_target(key, part):
    return tile_plan(key)[2]


def block_levels(key, shape, cuts, least, top_value):
    loudness, own = 1.0, jax.random.fold_in(key, 6)
    for dim, shards_of in cuts:
        heights = jnp.exp(jax.random.uniform(jax.random.fold_in(own, dim), (shards_of,), jnp.float32, least / len(cuts), top_value / len(cuts)))
        loudness = loudness * jnp.repeat(heights, shape[dim] // shards_of).reshape([-1 if axis == dim else 1 for axis in range(len(shape))])
    return loudness


def setup_inputs(seed: int = 0) -> dict:
    keys = jax.random.split(jax.random.key(seed), 9)
    return {
        "source_cells": draw_source_cells(jax.random.fold_in(keys[8], 71), 0),
        "target_cells": draw_target_cells(jax.random.fold_in(keys[8], 71), 0),
        "mapping": draw_mapping(jax.random.fold_in(keys[8], 71), 0),
        "source_logmass": jnp.clip(jax.random.uniform(keys[3], (NS,), jnp.float32, -1.0, 1.0) * block_levels(keys[3], (NS,), ((0, 256),), -0.4, 0.0), -1.0, 1.0).astype(jnp.bfloat16),
        "target_logmass": jnp.clip(jax.random.uniform(keys[4], (NT,), jnp.float32, -1.0, 1.0) * block_levels(keys[4], (NT,), ((0, 64),), -0.4, 0.0), -1.0, 1.0).astype(jnp.bfloat16),
        "group_blocks": draw_group_blocks(jax.random.fold_in(keys[8], 71), 0),
        "tile_source": draw_tile_source(jax.random.fold_in(keys[8], 71), 0),
        "tile_target": draw_tile_target(jax.random.fold_in(keys[8], 71), 0),
    }


entropy = 0.5
damping = 0.8
lowest_score = -1e+30

def reference(source_cells, target_cells, mapping, source_logmass, target_logmass, group_blocks, tile_source, tile_target):
    devices_all = N_SRC * N_TGT
    source_blocks = NS // TILE
    target_blocks = NT // TILE
    inverse_root = 1.0 / math.sqrt(D)
    mapped = jnp.dot(source_cells, mapping, preferred_element_type=jnp.float32).astype(jnp.bfloat16)
    device_index = jnp.arange(devices_all, dtype=jnp.int32)
    live_slot = tile_source >= 0
    source_block = jnp.where(live_slot, (device_index // N_TGT)[:, None] * N_TGT + tile_source, 0).astype(jnp.int32)
    target_block = jnp.where(live_slot, (device_index % N_TGT)[:, None] * TB_DEV + tile_target, 0).astype(jnp.int32)
    mapped_tiles = mapped.reshape(source_blocks, TILE, D)
    target_tiles = target_cells.reshape(target_blocks, TILE, D)

    def device_costs(pair):
        left_block, right_block = pair
        product = jnp.einsum('kid,kjd->kij', mapped_tiles[left_block].astype(jnp.float32), target_tiles[right_block].astype(jnp.float32))
        return product * -inverse_root
    costs = lax.map(device_costs, (source_block, target_block)).reshape(devices_all * TILES, TILE, TILE)
    flat_source = source_block.reshape(-1)
    flat_target = target_block.reshape(-1)
    flat_live = live_slot.reshape(-1)
    block_group = jnp.arange(source_blocks, dtype=jnp.int32) // N_TGT
    block_live = jnp.arange(source_blocks, dtype=jnp.int32) % N_TGT < group_blocks[block_group]
    row_live = jnp.repeat(block_live, TILE)
    source_logs = source_logmass.astype(jnp.float32)
    target_logs = target_logmass.astype(jnp.float32)

    def source_update(target_field):
        scores = (target_field.reshape(target_blocks, TILE)[flat_target][:, None, :] - costs) / entropy
        scores = jnp.where(flat_live[:, None, None], scores, lowest_score)
        block_max = jax.ops.segment_max(lax.optimization_barrier(jnp.max(scores, axis=2)), flat_source, num_segments=source_blocks)
        totals = lax.optimization_barrier(jnp.sum(jnp.exp(scores - block_max[flat_source][:, :, None]), axis=2))
        block_total = jax.ops.segment_sum(jnp.where(flat_live[:, None], totals, 0.0), flat_source, num_segments=source_blocks)
        safe_total = jnp.where(row_live, block_total.reshape(-1), 1.0)
        safe_max = jnp.where(row_live, block_max.reshape(-1), 0.0)
        return jnp.where(row_live, entropy * source_logs - entropy * (safe_max + jnp.log(safe_total)), 0.0)

    def target_update(source_field):
        scores = (source_field.reshape(source_blocks, TILE)[flat_source][:, :, None] - costs) / entropy
        scores = jnp.where(flat_live[:, None, None], scores, lowest_score)
        block_max = jax.ops.segment_max(lax.optimization_barrier(jnp.max(scores, axis=1)), flat_target, num_segments=target_blocks)
        totals = lax.optimization_barrier(jnp.sum(jnp.exp(scores - block_max[flat_target][:, None, :]), axis=1))
        block_total = jax.ops.segment_sum(jnp.where(flat_live[:, None], totals, 0.0), flat_target, num_segments=target_blocks)
        return entropy * target_logs - entropy * (block_max.reshape(-1) + jnp.log(block_total.reshape(-1)))
    target_field = jnp.zeros((NT,), jnp.float32)
    source_field = jnp.zeros((NS,), jnp.float32)
    for sweep_index in range(SINK):
        source_field = source_update(target_field)
        target_field = target_update(source_field)
    source_rows_of = source_field.reshape(source_blocks, TILE)[flat_source]
    target_rows_of = target_field.reshape(target_blocks, TILE)[flat_target]
    exponent = (source_rows_of[:, :, None] + target_rows_of[:, None, :] - costs) / entropy
    transport = jnp.where(flat_live[:, None, None], jnp.exp(jnp.where(flat_live[:, None, None], exponent, 0.0)), 0.0)
    row_mass = jax.ops.segment_sum(lax.optimization_barrier(jnp.sum(transport, axis=2)), flat_source, num_segments=source_blocks).reshape(-1)
    row_cost = jax.ops.segment_sum(lax.optimization_barrier(jnp.sum(transport * costs, axis=2)), flat_source, num_segments=source_blocks).reshape(-1) / entropy
    column_mass = jax.ops.segment_sum(lax.optimization_barrier(jnp.sum(transport, axis=1)), flat_target, num_segments=target_blocks).reshape(-1)
    column_cost = jax.ops.segment_sum(lax.optimization_barrier(jnp.sum(transport * costs, axis=1)), flat_target, num_segments=target_blocks).reshape(-1) / entropy
    safe_mass = jnp.where(row_live, row_mass, 1.0)
    target_ratio = jnp.zeros((NT,), jnp.float32)
    source_ratio = jnp.zeros((NS,), jnp.float32)
    for adjoint_index in range(ADJ):
        pulled = jnp.einsum('nij,nj->ni', transport, target_ratio.reshape(target_blocks, TILE)[flat_target])
        row_term = jax.ops.segment_sum(pulled, flat_source, num_segments=source_blocks).reshape(-1)
        source_ratio = jnp.where(row_live, (row_cost - damping * row_term) / safe_mass, 0.0)
        pushed = jnp.einsum('nij,ni->nj', transport, source_ratio.reshape(source_blocks, TILE)[flat_source])
        column_term = jax.ops.segment_sum(pushed, flat_target, num_segments=target_blocks).reshape(-1)
        target_ratio = (column_cost - damping * column_term) / column_mass
    weights = transport * (1.0 - costs / entropy + source_ratio.reshape(source_blocks, TILE)[flat_source][:, :, None] + target_ratio.reshape(target_blocks, TILE)[flat_target][:, None, :])
    weights = weights.astype(jnp.bfloat16).reshape(devices_all, TILES, TILE, TILE)

    def accumulate(carry, item):
        device_weights, device_source, device_target = item
        products = jnp.einsum('kij,kjd->kid', device_weights.astype(jnp.float32), target_tiles[device_target].astype(jnp.float32))
        return (carry.at[device_source].add(products), None)
    row_products, unused = lax.scan(accumulate, jnp.zeros((source_blocks, TILE, D), jnp.float32), (weights, source_block, target_block))
    map_gradient = jnp.dot(source_cells.astype(jnp.float32).T, row_products.reshape(NS, D), precision=lax.Precision.HIGHEST) * -inverse_root
    return (source_field, target_field, map_gradient)
```

```python
import functools
import math

import jax
import jax.numpy as jnp
from jax import lax
from jax.experimental import pallas as pl
from jax.experimental.pallas import tpu as pltpu
from jax.sharding import Mesh, PartitionSpec as P

TILE = 128
TB_DEV = 8
TILES = 64
SINK = 4
ADJ = 4
D = 256

entropy = 0.5
damping = 0.8
lowest = -1e30

AXES = ("src", "x", "zh", "zl", "core")
ROW = ("x", "zh")
COL = ("src", "zl", "core")
NA = 16
NB = 32
SLOTS = 4 * TILES
CHUNK = 8
CHUNKS = SLOTS // CHUNK
F32 = jnp.float32


VM = pl.BlockSpec(memory_space=pltpu.VMEM)
SM = pl.BlockSpec(memory_space=pltpu.SMEM)
ANY = pl.BlockSpec(memory_space=pl.ANY)
SHAPE = jax.ShapeDtypeStruct
TILE_BUF = pltpu.VMEM((SLOTS, TILE, TILE), F32)
SEMS = pltpu.SemaphoreType.DMA((CHUNKS,))


def call(kernel, name, ins, outs, scratch, flops=2 << 20, moved=4 << 20, vmem=52):
    in_specs = [spec for spec, _ in ins]
    args = [value for _, value in ins]
    return pl.pallas_call(
        kernel,
        out_shape=[shape for _, shape in outs],
        in_specs=in_specs,
        out_specs=[spec for spec, _ in outs],
        scratch_shapes=scratch,
        name=name,
        cost_estimate=pl.CostEstimate(flops=flops, bytes_accessed=moved, transcendentals=0),
        compiler_params=pltpu.CompilerParams(vmem_limit_bytes=vmem << 20),
    )(*args)


def row_form(block):
    return jnp.sum(block.T, axis=0, keepdims=True)


def column_form(row):
    return jnp.broadcast_to(row, (TILE, TILE)).T


def fold(block):
    return jnp.sum(block.reshape(16, 8, TILE), axis=0)


def fold_max(block):
    return jnp.max(block.reshape(16, 8, TILE), axis=0)


def chunks_of(list_ref):
    return lax.shift_right_logical(list_ref[SLOTS] + (CHUNK - 1), 3)


def copies(source, buffer, sems, count, act):
    def one(c, carry):
        at = pl.ds(pl.multiple_of(c * CHUNK, CHUNK), CHUNK)
        copy = pltpu.make_async_copy(source.at[at], buffer.at[at], sems.at[c])
        getattr(copy, act)()
        return carry

    lax.fori_loop(0, count, one, 0)


def wait_chunk(source, buffer, sems, c):
    at = pl.ds(pl.multiple_of(c * CHUNK, CHUNK), CHUNK)
    pltpu.make_async_copy(source.at[at], buffer.at[at], sems.at[c]).wait()


def each_tile(list_ref, count, body, before=None, after=None):
    def one(c, carry):
        if before is not None:
            before(c)
        for step in range(CHUNK):
            k = c * CHUNK + step
            code = list_ref[k]
            body(k, lax.shift_right_logical(code, 5), jnp.bitwise_and(code, NB - 1))
        if after is not None:
            after(c)
        return carry

    lax.fori_loop(0, count, one, 0)


def write_copies(out_ref, rows, value, first=0):
    for d in range(16):
        out_ref[d, first : first + rows] = value


def live_rows(meta_ref):
    block = 4 * lax.broadcasted_iota(jnp.int32, (NA, TILE), 0) + meta_ref[1]
    return block < meta_ref[0]


def total(recv_ref, first, rows):
    so_far = recv_ref[0, first : first + rows]
    for d in range(1, 16):
        so_far = so_far + recv_ref[d, first : first + rows]
    return so_far


def merged(recv_ref, rows):
    largest = recv_ref[0, 0:rows]
    for d in range(1, 16):
        largest = jnp.maximum(largest, recv_ref[d, 0:rows])
    so_far = jnp.zeros((rows, TILE), F32)
    for d in range(16):
        so_far = so_far + jnp.exp(recv_ref[d, 0:rows] - largest)
    return largest + jnp.log(so_far)


def finish_log(largest, so_far):
    good = so_far > 0
    return jnp.where(good, largest + jnp.log(jnp.where(good, so_far, 1.0)), lowest)


def scores_kernel(
    codes_ref, meta_ref, cells_ref, t0, t1, t23, mapping_ref, mass_ref,
    send_ref, list_ref, x_any,
    tbuf, mapped, xbuf, top, acc, tsem, xsems,
):
    pulls = [
        pltpu.make_async_copy(t0, tbuf.at[0], tsem.at[0]),
        pltpu.make_async_copy(t1, tbuf.at[2], tsem.at[1]),
        pltpu.make_async_copy(t23.at[0], tbuf.at[1], tsem.at[2]),
        pltpu.make_async_copy(t23.at[1], tbuf.at[3], tsem.at[3]),
    ]
    for pull in pulls:
        pull.start()
    part = meta_ref[1]

    def gather(k, n):
        code = codes_ref[k]
        source = lax.shift_right_arithmetic(code, 3)
        take = jnp.logical_and(code >= 0, jnp.bitwise_and(source, 3) == part)
        owner = jnp.bitwise_xor(lax.shift_right_logical(k, 6), part)
        target = owner * TB_DEV + jnp.bitwise_and(code, TB_DEV - 1)
        packed = lax.shift_right_arithmetic(source, 2) * NB + target
        list_ref[n] = jnp.where(take, packed, 0)
        return n + jnp.where(take, 1, 0)

    count = lax.fori_loop(0, SLOTS, gather, 0)

    def clear(k, carry):
        list_ref[k] = 0
        return carry

    lax.fori_loop(count, jnp.minimum(count + CHUNK, SLOTS), clear, 0)
    list_ref[SLOTS] = count
    chunks = chunks_of(list_ref)

    def blank(a, carry):
        top[a] = jnp.full((TILE, TILE), lowest, F32)
        acc[a] = jnp.zeros((TILE, TILE), F32)
        product = jnp.dot(cells_ref[a], mapping_ref[...], preferred_element_type=F32)
        mapped[a] = product.astype(jnp.bfloat16)
        return carry

    lax.fori_loop(0, NA, blank, 0)
    for pull in pulls:
        pull.wait()
    scale = (1.0 / entropy) / math.sqrt(D)

    def product(k, a, b):
        slot = jnp.bitwise_xor(lax.shift_right_logical(b, 3), part)
        rows = pl.ds(pl.multiple_of(jnp.bitwise_and(b, TB_DEV - 1) * TILE, TILE), TILE)
        x = lax.dot_general(
            mapped[a], tbuf[slot, rows, :], (((1,), (1,)), ((), ())), preferred_element_type=F32
        )
        x = jnp.where(k < count, x * scale, lowest)
        xbuf[k] = x
        top[a] = jnp.maximum(top[a], x)

    def push(c):
        at = pl.ds(pl.multiple_of(c * CHUNK, CHUNK), CHUNK)
        pltpu.make_async_copy(xbuf.at[at], x_any.at[at], xsems.at[c]).start()

    each_tile(list_ref, chunks, product, after=push)

    def spread(a, carry):
        top[a] = jnp.broadcast_to(jnp.max(top[a], axis=1, keepdims=True), (TILE, TILE))
        return carry

    lax.fori_loop(0, NA, spread, 0)

    def add(k, a, b):
        acc[a] += jnp.exp(xbuf[k] - top[a])

    each_tile(list_ref, chunks, add)
    for a in range(NA):
        row = finish_log(top[a].T[0:1], row_form(acc[a]))
        for d in range(16):
            send_ref[d, a : a + 1] = row
    tail = jnp.broadcast_to(mass_ref[...], (8, TILE))
    write_copies(send_ref, 8, tail, NA)
    copies(xbuf, x_any, xsems, chunks, "wait")


def first_targets_kernel(
    list_ref, meta_ref, recv_ref, x_any, mass_ref,
    send_ref, u_ref, mass_out,
    xbuf, col, top, acc, sems,
):
    chunks = chunks_of(list_ref)
    copies(x_any, xbuf, sems, chunks, "start")
    for a in range(NA):
        mass_out[a : a + 1] = recv_ref[a, NA : NA + 1]
    u = jnp.where(live_rows(meta_ref), mass_out[...] - merged(recv_ref, NA), 0.0)
    u_ref[...] = u
    for a in range(NA):
        col[a] = column_form(u[a : a + 1])
    top[...] = jnp.full((NB, 8, TILE), lowest, F32)
    acc[...] = jnp.zeros((NB, 8, TILE), F32)

    def largest(k, a, b):
        y = xbuf[k] + col[a]
        xbuf[k] = y
        top[b] = jnp.maximum(top[b], fold_max(y))

    each_tile(list_ref, chunks, largest, before=functools.partial(wait_chunk, x_any, xbuf, sems))
    for b in range(NB):
        top[b] = jnp.broadcast_to(jnp.max(top[b], axis=0, keepdims=True), (8, TILE))

    def add(k, a, b):
        acc[b] += fold(jnp.exp(xbuf[k] - top[b][0:1]))

    each_tile(list_ref, chunks, add)
    for b in range(NB):
        row = finish_log(top[b][0:1], jnp.sum(acc[b], axis=0, keepdims=True))
        for d in range(16):
            send_ref[d, b : b + 1] = row
    write_copies(send_ref, TB_DEV, mass_ref[...], NB)


def kernel_matrix_kernel(
    list_ref, recv_ref, u_ref, x_any,
    send_ref, v_ref, mass_out, k_any,
    xbuf, col, acc, sems, ksems,
):
    chunks = chunks_of(list_ref)
    copies(x_any, xbuf, sems, chunks, "start")
    for p in range(4):
        mass_out[p * TB_DEV : (p + 1) * TB_DEV] = recv_ref[p, NB : NB + TB_DEV]
    v_ref[...] = mass_out[...] - merged(recv_ref, NB)
    for a in range(NA):
        col[a] = column_form(u_ref[a : a + 1])
    acc[...] = jnp.zeros((NA, TILE, TILE), F32)

    def build(k, a, b):
        value = jnp.exp(xbuf[k] + col[a] + v_ref[pl.ds(b, 1)])
        xbuf[k] = value
        acc[a] += value

    def push(c):
        at = pl.ds(pl.multiple_of(c * CHUNK, CHUNK), CHUNK)
        pltpu.make_async_copy(xbuf.at[at], k_any.at[at], ksems.at[c]).start()

    each_tile(
        list_ref, chunks, build, before=functools.partial(wait_chunk, x_any, xbuf, sems), after=push
    )
    for a in range(NA):
        row = row_form(acc[a])
        for d in range(16):
            send_ref[d, a : a + 1] = row
    copies(xbuf, k_any, ksems, chunks, "wait")


def columns_kernel(list_ref, meta_ref, recv_ref, mass_ref, k_any, send_ref, alpha_ref, kbuf, col, acc, sems):
    chunks = chunks_of(list_ref)
    copies(k_any, kbuf, sems, chunks, "start")
    alpha = jnp.where(live_rows(meta_ref), jnp.exp(mass_ref[...]) / total(recv_ref, 0, NA), 1.0)
    alpha_ref[...] = alpha
    for a in range(NA):
        col[a] = column_form(alpha[a : a + 1])
    acc[...] = jnp.zeros((NB, 8, TILE), F32)

    def add(k, a, b):
        acc[b] += fold(kbuf[k] * col[a])

    each_tile(list_ref, chunks, add, before=functools.partial(wait_chunk, k_any, kbuf, sems))
    write_copies(send_ref, NB, jnp.sum(acc[...], axis=1))


def rows_kernel(list_ref, recv_ref, mass_ref, k_any, send_ref, beta_ref, kbuf, acc, sems):
    chunks = chunks_of(list_ref)
    copies(k_any, kbuf, sems, chunks, "start")
    beta_ref[...] = jnp.exp(mass_ref[...]) / total(recv_ref, 0, NB)
    acc[...] = jnp.zeros((NA, TILE, TILE), F32)

    def add(k, a, b):
        acc[a] += kbuf[k] * beta_ref[pl.ds(b, 1)]

    each_tile(list_ref, chunks, add, before=functools.partial(wait_chunk, k_any, kbuf, sems))
    for a in range(NA):
        row = row_form(acc[a])
        for d in range(16):
            send_ref[d, a : a + 1] = row


def masses_kernel(
    list_ref, recv_ref, mass_ref, k_any, x_any,
    send_ref, beta_ref, sum_ref, cost_ref,
    kbuf, xbuf, acc, acc_cost, sems, xsems,
):
    chunks = chunks_of(list_ref)
    copies(k_any, kbuf, sems, chunks, "start")
    copies(x_any, xbuf, xsems, chunks, "start")
    column_sum = total(recv_ref, 0, NB)
    sum_ref[...] = column_sum
    beta_ref[...] = jnp.exp(mass_ref[...]) / column_sum
    acc[...] = jnp.zeros((NA, TILE, TILE), F32)
    acc_cost[...] = jnp.zeros((NA, TILE, TILE), F32)

    def ready(c):
        wait_chunk(k_any, kbuf, sems, c)
        wait_chunk(x_any, xbuf, xsems, c)

    def add(k, a, b):
        plan = kbuf[k] * beta_ref[pl.ds(b, 1)]
        acc[a] += plan
        acc_cost[a] += plan * xbuf[k]

    each_tile(list_ref, chunks, add, before=ready)
    for a in range(NA):
        row = row_form(acc[a])
        cost = row_form(acc_cost[a])
        cost_ref[a : a + 1] = cost
        for d in range(16):
            send_ref[d, a : a + 1] = row
            send_ref[d, NA + a : NA + a + 1] = cost


def first_ratio_kernel(
    list_ref, meta_ref, recv_ref, alpha_ref, k_any, x_any,
    send_ref, sum_ref, s_ref, cost_ref,
    kbuf, xbuf, col, col2, acc, acc2, sems, xsems,
):
    chunks = chunks_of(list_ref)
    copies(k_any, kbuf, sems, chunks, "start")
    copies(x_any, xbuf, xsems, chunks, "start")
    row_sum = total(recv_ref, 0, NA)
    sum_ref[...] = row_sum
    s = jnp.where(live_rows(meta_ref), -total(recv_ref, NA, NA) / row_sum, 0.0)
    s_ref[...] = s
    for a in range(NA):
        col[a] = column_form(alpha_ref[a : a + 1])
        col2[a] = column_form(s[a : a + 1] * damping)
    acc[...] = jnp.zeros((NB, 8, TILE), F32)
    acc2[...] = jnp.zeros((NB, 8, TILE), F32)

    def ready(c):
        wait_chunk(k_any, kbuf, sems, c)
        wait_chunk(x_any, xbuf, xsems, c)

    def add(k, a, b):
        plan = kbuf[k] * col[a]
        acc[b] += fold(plan * xbuf[k])
        acc2[b] += fold(plan * (xbuf[k] + col2[a]))

    each_tile(list_ref, chunks, add, before=ready)
    cost_ref[...] = jnp.sum(acc[...], axis=1)
    write_copies(send_ref, NB, jnp.sum(acc2[...], axis=1))


def pull_kernel(
    list_ref, recv_ref, sum_ref, beta_ref, cost_ref, k_any,
    send_ref,
    kbuf, acc, weight, sems,
):
    chunks = chunks_of(list_ref)
    copies(k_any, kbuf, sems, chunks, "start")
    t = -total(recv_ref, 0, NB) / sum_ref[...]
    weight[...] = beta_ref[...] * t * damping
    acc[...] = jnp.zeros((NA, TILE, TILE), F32)

    def add(k, a, b):
        acc[a] += kbuf[k] * weight[pl.ds(b, 1)]

    each_tile(list_ref, chunks, add, before=functools.partial(wait_chunk, k_any, kbuf, sems))
    for a in range(NA):
        row = cost_ref[a : a + 1] + row_form(acc[a])
        for d in range(16):
            send_ref[d, a : a + 1] = row


def push_kernel(
    list_ref, meta_ref, recv_ref, sum_ref, alpha_ref, cost_ref, k_any,
    send_ref, s_ref,
    kbuf, col, acc, sems,
):
    chunks = chunks_of(list_ref)
    copies(k_any, kbuf, sems, chunks, "start")
    s = jnp.where(live_rows(meta_ref), -total(recv_ref, 0, NA) / sum_ref[...], 0.0)
    s_ref[...] = s
    weight = alpha_ref[...] * s * damping
    for a in range(NA):
        col[a] = column_form(weight[a : a + 1])
    acc[...] = jnp.zeros((NB, 8, TILE), F32)

    def add(k, a, b):
        acc[b] += fold(kbuf[k] * col[a])

    each_tile(list_ref, chunks, add, before=functools.partial(wait_chunk, k_any, kbuf, sems))
    write_copies(send_ref, NB, cost_ref[...] + jnp.sum(acc[...], axis=1))


def gradient_kernel(
    list_ref, meta_ref, recv_ref, sum_ref, beta_ref, alpha_ref, s_ref, cells_ref, t0, t1, t23, k_any, x_any,
    g_ref,
    tbuf, kbuf, xbuf, col, col2, trow, prod, tsem, sems, xsems,
):
    chunks = chunks_of(list_ref)
    pulls = [
        pltpu.make_async_copy(t0, tbuf.at[0], tsem.at[0]),
        pltpu.make_async_copy(t1, tbuf.at[2], tsem.at[1]),
        pltpu.make_async_copy(t23.at[0], tbuf.at[1], tsem.at[2]),
        pltpu.make_async_copy(t23.at[1], tbuf.at[3], tsem.at[3]),
    ]
    for pull in pulls:
        pull.start()
    copies(k_any, kbuf, sems, chunks, "start")
    copies(x_any, xbuf, xsems, chunks, "start")
    part = meta_ref[1]
    trow[...] = -total(recv_ref, 0, NB) / sum_ref[...]
    for a in range(NA):
        col[a] = column_form(alpha_ref[a : a + 1])
        col2[a] = column_form(1.0 + s_ref[a : a + 1])
    prod[...] = jnp.zeros((NA, TILE, D), F32)
    for pull in pulls:
        pull.wait()

    def ready(c):
        wait_chunk(k_any, kbuf, sems, c)
        wait_chunk(x_any, xbuf, xsems, c)

    def add(k, a, b):
        slot = jnp.bitwise_xor(lax.shift_right_logical(b, 3), part)
        rows = pl.ds(pl.multiple_of(jnp.bitwise_and(b, TB_DEV - 1) * TILE, TILE), TILE)
        plan = kbuf[k] * col[a] * beta_ref[pl.ds(b, 1)]
        weights = plan * (xbuf[k] + col2[a] + trow[pl.ds(b, 1)])
        prod[a] += jnp.dot(
            weights.astype(jnp.bfloat16), tbuf[slot, rows, :], preferred_element_type=F32
        )

    each_tile(list_ref, chunks, add, before=ready)
    contract = (((0,), (0,)), ((), ()))

    def outer(a, so_far):
        value = prod[a]
        high = value.astype(jnp.bfloat16)
        rest = value - high.astype(F32)
        middle = rest.astype(jnp.bfloat16)
        low = (rest - middle.astype(F32)).astype(jnp.bfloat16)
        cells = cells_ref[a]
        for piece in (low, middle, high):
            so_far = so_far + lax.dot_general(cells, piece, contract, preferred_element_type=F32)
        return so_far

    g = lax.fori_loop(0, NA, outer, jnp.zeros((D, D), F32))
    g_ref[...] = g * (-1.0 / math.sqrt(D))


def swap(value, axis):
    return lax.ppermute(value, axis, [(0, 1), (1, 0)])


def shards(
    source_cells,
    target_cells,
    mapping,
    source_logmass,
    target_logmass,
    group_blocks,
    tile_source,
    tile_target,
):
    part = lax.axis_index("zl") * 2 + lax.axis_index("core")
    owner = lax.axis_index("x") * 4 + lax.axis_index("zh")
    live = group_blocks[lax.axis_index("src")]
    meta = jnp.stack([live, part]).astype(jnp.int32)

    codes = jnp.where(tile_source >= 0, tile_source * TB_DEV + tile_target, -1)
    codes_zl = swap(codes, "zl")
    codes_core = swap(jnp.concatenate([codes, codes_zl], axis=1), "core")
    codes_all = jnp.concatenate([codes, codes_core[:, :TILES], codes_zl, codes_core[:, TILES:]], axis=1)
    t0 = target_cells
    t1 = swap(target_cells, "zl")
    t23 = swap(jnp.stack([t0, t1]), "core")
    cells = lax.all_to_all(jnp.broadcast_to(source_cells[None], (16, TILE, D)), ROW, 0, 0)

    def row_exchange(value):
        return lax.all_to_all(value, ROW, 0, 0)

    def col_exchange(value):
        return lax.all_to_all(value, COL, 0, 0)

    rows_to = (VM, SHAPE((16, NA, TILE), F32))
    cols_to = (VM, SHAPE((16, NB, TILE), F32))
    rows_state = (VM, SHAPE((NA, TILE), F32))
    cols_state = (VM, SHAPE((NB, TILE), F32))
    tiles = (ANY, SHAPE((SLOTS, TILE, TILE), F32))
    row_blocks = pltpu.VMEM((NA, TILE, TILE), F32)
    col_rows = pltpu.VMEM((NB, 8, TILE), F32)

    send, tile_list, x = call(
        scores_kernel,
        "scores",
        [
            (SM, codes_all.reshape(SLOTS)), (SM, meta), (VM, cells), (ANY, t0), (ANY, t1), (ANY, t23),
            (VM, mapping), (VM, source_logmass.astype(F32).reshape(1, TILE)),
        ],
        [(VM, SHAPE((16, NA + 8, TILE), F32)), (SM, SHAPE((SLOTS + 8,), jnp.int32)), tiles],
        [
            pltpu.VMEM((4, TB_DEV * TILE, D), jnp.bfloat16), pltpu.VMEM((NA, TILE, D), jnp.bfloat16),
            TILE_BUF, row_blocks, row_blocks, pltpu.SemaphoreType.DMA((4,)), SEMS,
        ],
        moved=8 << 20,
    )
    recv = row_exchange(send)
    send, u, source_mass = call(
        first_targets_kernel,
        "first_targets",
        [
            (SM, tile_list), (SM, meta), (VM, recv), (ANY, x),
            (VM, target_logmass.astype(F32).reshape(TB_DEV, TILE)),
        ],
        [(VM, SHAPE((16, NB + TB_DEV, TILE), F32)), rows_state, rows_state],
        [TILE_BUF, row_blocks, col_rows, col_rows, SEMS],
    )
    recv = col_exchange(send)
    send, v, target_mass, k = call(
        kernel_matrix_kernel,
        "kernel_matrix",
        [(SM, tile_list), (VM, recv), (VM, u), (ANY, x)],
        [rows_to, cols_state, cols_state, tiles],
        [TILE_BUF, row_blocks, row_blocks, SEMS, SEMS],
        moved=8 << 20,
    )
    for sweep in range(1, SINK):
        recv = row_exchange(send)
        send, alpha = call(
            columns_kernel,
            "columns",
            [(SM, tile_list), (SM, meta), (VM, recv), (VM, source_mass), (ANY, k)],
            [cols_to, rows_state],
            [TILE_BUF, row_blocks, col_rows, SEMS],
        )
        recv = col_exchange(send)
        if sweep < SINK - 1:
            send, _ = call(
                rows_kernel,
                "rows",
                [(SM, tile_list), (VM, recv), (VM, target_mass), (ANY, k)],
                [rows_to, cols_state],
                [TILE_BUF, row_blocks, SEMS],
            )
    send, beta, column_sum, row_cost = call(
        masses_kernel,
        "masses",
        [(SM, tile_list), (VM, recv), (VM, target_mass), (ANY, k), (ANY, x)],
        [(VM, SHAPE((16, 2 * NA, TILE), F32)), cols_state, cols_state, rows_state],
        [TILE_BUF, TILE_BUF, row_blocks, row_blocks, SEMS, SEMS],
        moved=8 << 20,
    )
    recv = row_exchange(send)
    send, row_sum, s, column_cost = call(
        first_ratio_kernel,
        "first_ratio",
        [(SM, tile_list), (SM, meta), (VM, recv), (VM, alpha), (ANY, k), (ANY, x)],
        [cols_to, rows_state, rows_state, cols_state],
        [TILE_BUF, TILE_BUF, row_blocks, row_blocks, col_rows, col_rows, SEMS, SEMS],
        moved=8 << 20,
    )
    recv = col_exchange(send)
    for _ in range(1, ADJ):
        (send,) = call(
            pull_kernel,
            "pull",
            [(SM, tile_list), (VM, recv), (VM, column_sum), (VM, beta), (VM, row_cost), (ANY, k)],
            [rows_to],
            [TILE_BUF, row_blocks, pltpu.VMEM((NB, TILE), F32), SEMS],
        )
        recv = row_exchange(send)
        send, s = call(
            push_kernel,
            "push",
            [
                (SM, tile_list), (SM, meta), (VM, recv), (VM, row_sum), (VM, alpha),
                (VM, column_cost), (ANY, k),
            ],
            [cols_to, rows_state],
            [TILE_BUF, row_blocks, col_rows, SEMS],
        )
        recv = col_exchange(send)
    (gradient,) = call(
        gradient_kernel,
        "gradient",
        [
            (SM, tile_list), (SM, meta), (VM, recv), (VM, column_sum), (VM, beta), (VM, alpha), (VM, s),
            (VM, cells), (ANY, t0), (ANY, t1), (ANY, t23), (ANY, k), (ANY, x),
        ],
        [(VM, SHAPE((D, D), F32))],
        [
            pltpu.VMEM((4, TB_DEV * TILE, D), jnp.bfloat16), TILE_BUF, TILE_BUF, row_blocks, row_blocks,
            pltpu.VMEM((NB, TILE), F32), pltpu.VMEM((NA, TILE, D), F32),
            pltpu.SemaphoreType.DMA((4,)), SEMS, SEMS,
        ],
        moved=10 << 20,
    )
    piece = jnp.sum(col_exchange(gradient.reshape(16, 16, D)), axis=0)
    piece = jnp.sum(row_exchange(jnp.broadcast_to(piece[None], (16, 16, D))), axis=0)
    map_gradient = col_exchange_gather(piece).reshape(D, D)

    source_field = entropy * (u + jnp.log(alpha))
    own_source = lax.dynamic_slice_in_dim(source_field, owner, 1, 0).reshape(TILE)
    target_field = entropy * (v + jnp.log(beta))
    own_target = lax.dynamic_slice_in_dim(target_field, part * TB_DEV, TB_DEV, 0)
    return (own_source, own_target.reshape(TB_DEV * TILE), map_gradient)


def col_exchange_gather(piece):
    every = lax.all_to_all(jnp.broadcast_to(piece[None], (16, 16, D)), COL, 0, 0)
    return every


def solution(mesh):
    grid = Mesh(mesh.devices.reshape(4, 4, 4, 2, 2), AXES)
    tgt = ("x", "zh", "zl", "core")
    both = ("src", *tgt)
    in_specs = (
        P(both, None),
        P(tgt, None),
        P(),
        P(both),
        P(tgt),
        P(),
        P(both, None),
        P(both, None),
    )
    out_specs = (P(both), P(tgt), P())
    return jax.shard_map(shards, mesh=grid, in_specs=in_specs, out_specs=out_specs, check_vma=False)
```

```python
import math

import jax
import jax.numpy as jnp
from jax import lax
from jax.experimental import pallas as pl
from jax.experimental.pallas import tpu as pltpu
from jax.sharding import Mesh, PartitionSpec as P

TILE = 128
TB_DEV = 8
TILES = 64
SINK = 4
ADJ = 4
D = 256

entropy = 0.5
damping = 0.8
lowest = -1e30

AXES = ("src", "x", "zh", "zl", "core")
ROW = ("x", "zh")
COL = ("src", "zl", "core")
NA = 16
NB = 32
SLOTS = 4 * TILES
CHUNK = 8
F32 = jnp.float32


VM = pl.BlockSpec(memory_space=pltpu.VMEM)
SM = pl.BlockSpec(memory_space=pltpu.SMEM)
ANY = pl.BlockSpec(memory_space=pl.ANY)
SHAPE = jax.ShapeDtypeStruct


HERE = "here"
FAR = "far"


def call(kernel, name, ins, outs, scratch, flops=2 << 20, moved=1 << 20, vmem=9):
    in_specs, args = [], []
    for spec, value in ins:
        if spec in (HERE, FAR):
            space = pltpu.VMEM if spec == HERE else pltpu.HBM
            spec, value = pl.BlockSpec(memory_space=space), pltpu.with_memory_space_constraint(value, space)
        in_specs.append(spec)
        args.append(value)
    outs = [(VM, pltpu.VMEM(shape.shape, shape.dtype)) if spec == HERE else (spec, shape) for spec, shape in outs]
    return pl.pallas_call(
        kernel,
        out_shape=[shape for _, shape in outs],
        in_specs=in_specs,
        out_specs=[spec for spec, _ in outs],
        scratch_shapes=scratch,
        name=name,
        cost_estimate=pl.CostEstimate(flops=flops, bytes_accessed=moved, transcendentals=0),
        compiler_params=pltpu.CompilerParams(vmem_limit_bytes=vmem << 20),
    )(*args)


def row_form(block):
    return jnp.sum(block.T, axis=0, keepdims=True)


def column_form(row):
    return jnp.broadcast_to(row, (TILE, TILE)).T


def fold(block):
    return jnp.sum(block.reshape(16, 8, TILE), axis=0)


def fold_max(block):
    return jnp.max(block.reshape(16, 8, TILE), axis=0)


def each_tile(list_ref, body):
    def one(c, carry):
        for step in range(CHUNK):
            k = c * CHUNK + step
            code = list_ref[k]
            body(k, lax.shift_right_logical(code, 5), jnp.bitwise_and(code, NB - 1))
        return carry

    lax.fori_loop(0, lax.shift_right_logical(list_ref[SLOTS] + (CHUNK - 1), 3), one, 0)


def part_index():
    return lax.axis_index("zl") * 2 + lax.axis_index("core")


def pulls_of(own_cells, more_cells, targets, cells, tbuf, sem):
    x, zh = lax.axis_index("x"), lax.axis_index("zh")
    pulls = [
        pltpu.make_async_copy(targets[0], tbuf.at[0], sem.at[0]),
        pltpu.make_async_copy(targets[1], tbuf.at[1], sem.at[1]),
        pltpu.make_async_copy(targets[2], tbuf.at[2], sem.at[2]),
        pltpu.make_async_copy(targets[3], tbuf.at[3], sem.at[3]),
    ]
    for m, piece in enumerate((own_cells, *more_cells)):
        for k in range(4):
            place = jnp.bitwise_and(x + (4 - m), 3) * 4 + jnp.bitwise_and(zh + (4 - k), 3)
            pulls.append(pltpu.make_async_copy(piece.at[k], cells.at[place], sem.at[4 + 4 * m + k]))
    return pulls


def write_copies(out_ref, rows, value, first=0):
    for d in range(16):
        out_ref[d, first : first + rows] = value


def live_rows(list_ref):
    block = 4 * lax.broadcasted_iota(jnp.int32, (NA, TILE), 0) + part_index()
    return block < list_ref[SLOTS + 1]


def total(recv_ref, first, rows):
    so_far = recv_ref[0, first : first + rows]
    for d in range(1, 16):
        so_far = so_far + recv_ref[d, first : first + rows]
    return so_far


def merged(recv_ref, rows):
    largest = recv_ref[0, 0:rows]
    for d in range(1, 16):
        largest = jnp.maximum(largest, recv_ref[d, 0:rows])
    so_far = jnp.zeros((rows, TILE), F32)
    for d in range(16):
        so_far = so_far + jnp.exp(recv_ref[d, 0:rows] - largest)
    return largest + jnp.log(so_far)


def finish_log(largest, so_far):
    good = so_far > 0
    return jnp.where(good, largest + jnp.log(jnp.where(good, so_far, 1.0)), lowest)


def scores_kernel(
    codes0, codes1, codes2, codes3, own_cells, c1, c2, c3, t0, t1, t2, t3, mapping_far, mass_ref,
    send_ref, list_ref, xbuf,
    tbuf, cells_ref, mapping_ref, mapped, top, acc, sem,
):
    pulls = pulls_of(own_cells, (c1, c2, c3), (t0, t1, t2, t3), cells_ref, tbuf, sem)
    pulls.append(pltpu.make_async_copy(mapping_far, mapping_ref, sem.at[20]))
    for pull in pulls:
        pull.start()
    part = part_index()
    count = 0
    for r, codes in enumerate((codes0, codes1, codes2, codes3)):
        base = jnp.bitwise_xor(part, r) * TB_DEV

        def gather(k, n, codes=codes, base=base):
            code = codes[0, k]
            source = lax.shift_right_arithmetic(code, 3)
            take = jnp.logical_and(code >= 0, jnp.bitwise_and(source, 3) == part)
            target = base + jnp.bitwise_and(code, TB_DEV - 1)
            list_ref[n] = lax.shift_right_arithmetic(source, 2) * NB + target
            return n + take.astype(jnp.int32)

        count = lax.fori_loop(0, TILES, gather, count, unroll=8)

    def clear(k, carry):
        list_ref[k] = 0
        return carry

    lax.fori_loop(count, jnp.minimum(count + CHUNK, SLOTS), clear, 0)
    list_ref[SLOTS] = count
    list_ref[SLOTS + 1] = codes0[0, TILES + lax.axis_index("src")]
    for pull in pulls:
        pull.wait()

    def blank(a, carry):
        top[a] = jnp.full((TILE, TILE), lowest, F32)
        acc[a] = jnp.zeros((TILE, TILE), F32)
        product = jnp.dot(cells_ref[a], mapping_ref[...], preferred_element_type=F32)
        mapped[a] = product.astype(jnp.bfloat16)
        return carry

    lax.fori_loop(0, NA, blank, 0)
    scale = (1.0 / entropy) / math.sqrt(D)

    def product(k, a, b):
        slot = jnp.bitwise_xor(lax.shift_right_logical(b, 3), part)
        rows = pl.ds(pl.multiple_of(jnp.bitwise_and(b, TB_DEV - 1) * TILE, TILE), TILE)
        x = lax.dot_general(
            mapped[a], tbuf[slot, rows, :], (((1,), (1,)), ((), ())), preferred_element_type=F32
        )
        x = jnp.where(k < count, x * scale, lowest)
        xbuf[k] = x
        top[a] = jnp.maximum(top[a], x)

    each_tile(list_ref, product)

    def spread(a, carry):
        top[a] = jnp.broadcast_to(jnp.max(top[a], axis=1, keepdims=True), (TILE, TILE))
        return carry

    lax.fori_loop(0, NA, spread, 0)

    def add(k, a, b):
        acc[a] += jnp.exp(xbuf[k] - top[a])

    each_tile(list_ref, add)
    for a in range(NA):
        row = finish_log(top[a].T[0:1], row_form(acc[a]))
        for d in range(16):
            send_ref[d, a : a + 1] = row
    write_copies(send_ref, 8, jnp.broadcast_to(mass_ref[...], (8, TILE)), NA)


def first_targets_kernel(
    list_ref, recv_ref, xbuf, mass_ref,
    send_ref, u_ref, mass_out,
    col, top, acc,
):
    for a in range(NA):
        mass_out[a : a + 1] = recv_ref[a, NA : NA + 1]
    u = jnp.where(live_rows(list_ref), mass_out[...] - merged(recv_ref, NA), 0.0)
    u_ref[...] = u
    for a in range(NA):
        col[a] = column_form(u[a : a + 1])
    top[...] = jnp.full((NB, 8, TILE), lowest, F32)
    acc[...] = jnp.zeros((NB, 8, TILE), F32)

    def largest(k, a, b):
        top[b] = jnp.maximum(top[b], fold_max(xbuf[k] + col[a]))

    each_tile(list_ref, largest)
    for b in range(NB):
        top[b] = jnp.broadcast_to(jnp.max(top[b], axis=0, keepdims=True), (8, TILE))

    def add(k, a, b):
        acc[b] += fold(jnp.exp(xbuf[k] + col[a] - top[b][0:1]))

    each_tile(list_ref, add)
    for b in range(NB):
        row = finish_log(top[b][0:1], jnp.sum(acc[b], axis=0, keepdims=True))
        for d in range(16):
            send_ref[d, b : b + 1] = row
    write_copies(send_ref, TB_DEV, mass_ref[...], NB)


def kernel_matrix_kernel(
    list_ref, recv_ref, u_ref, xbuf,
    send_ref, v_ref, mass_out, kbuf,
    col, acc,
):
    for p in range(4):
        mass_out[p * TB_DEV : (p + 1) * TB_DEV] = recv_ref[p, NB : NB + TB_DEV]
    v_ref[...] = mass_out[...] - merged(recv_ref, NB)
    for a in range(NA):
        col[a] = column_form(u_ref[a : a + 1])
    acc[...] = jnp.zeros((NA, TILE, TILE), F32)

    def build(k, a, b):
        value = jnp.exp(xbuf[k] + col[a] + v_ref[pl.ds(b, 1)])
        kbuf[k] = value
        acc[a] += value

    each_tile(list_ref, build)
    for a in range(NA):
        row = row_form(acc[a])
        for d in range(16):
            send_ref[d, a : a + 1] = row


def columns_kernel(list_ref, recv_ref, mass_ref, kbuf, _, send_ref, alpha_ref, col, acc):
    alpha = jnp.where(live_rows(list_ref), jnp.exp(mass_ref[...]) / total(recv_ref, 0, NA), 1.0)
    alpha_ref[...] = alpha
    for a in range(NA):
        col[a] = column_form(alpha[a : a + 1])
    acc[...] = jnp.zeros((NB, 8, TILE), F32)

    def add(k, a, b):
        acc[b] += fold(kbuf[k] * col[a])

    each_tile(list_ref, add)
    write_copies(send_ref, NB, jnp.sum(acc[...], axis=1))


def rows_kernel(list_ref, recv_ref, mass_ref, kbuf, _, send_ref, beta_ref, acc):
    beta_ref[...] = jnp.exp(mass_ref[...]) / total(recv_ref, 0, NB)
    acc[...] = jnp.zeros((NA, TILE, TILE), F32)

    def add(k, a, b):
        acc[a] += kbuf[k] * beta_ref[pl.ds(b, 1)]

    each_tile(list_ref, add)
    for a in range(NA):
        row = row_form(acc[a])
        for d in range(16):
            send_ref[d, a : a + 1] = row


def masses_kernel(
    list_ref, recv_ref, mass_ref, kbuf, xbuf,
    send_ref, beta_ref, sum_ref, cost_ref,
    acc, acc_cost,
):
    column_sum = total(recv_ref, 0, NB)
    sum_ref[...] = column_sum
    beta_ref[...] = jnp.exp(mass_ref[...]) / column_sum
    acc[...] = jnp.zeros((NA, TILE, TILE), F32)
    acc_cost[...] = jnp.zeros((NA, TILE, TILE), F32)

    def add(k, a, b):
        plan = kbuf[k] * beta_ref[pl.ds(b, 1)]
        acc[a] += plan
        acc_cost[a] += plan * xbuf[k]

    each_tile(list_ref, add)
    for a in range(NA):
        row = row_form(acc[a])
        cost = row_form(acc_cost[a])
        cost_ref[a : a + 1] = cost
        for d in range(16):
            send_ref[d, a : a + 1] = row
            send_ref[d, NA + a : NA + a + 1] = cost


def first_ratio_kernel(
    list_ref, recv_ref, alpha_ref, kbuf, xbuf,
    send_ref, sum_ref, s_ref, cost_ref,
    col, col2, acc, acc2,
):
    row_sum = total(recv_ref, 0, NA)
    sum_ref[...] = row_sum
    s = jnp.where(live_rows(list_ref), -total(recv_ref, NA, NA) / row_sum, 0.0)
    s_ref[...] = s
    for a in range(NA):
        col[a] = column_form(alpha_ref[a : a + 1])
        col2[a] = column_form(s[a : a + 1] * damping)
    acc[...] = jnp.zeros((NB, 8, TILE), F32)
    acc2[...] = jnp.zeros((NB, 8, TILE), F32)

    def add(k, a, b):
        plan = kbuf[k] * col[a]
        acc[b] += fold(plan * xbuf[k])
        acc2[b] += fold(plan * (xbuf[k] + col2[a]))

    each_tile(list_ref, add)
    cost_ref[...] = jnp.sum(acc[...], axis=1)
    write_copies(send_ref, NB, jnp.sum(acc2[...], axis=1))


def pull_kernel(
    list_ref, recv_ref, sum_ref, beta_ref, cost_ref, kbuf, _,
    send_ref,
    acc, weight,
):
    t = -total(recv_ref, 0, NB) / sum_ref[...]
    weight[...] = beta_ref[...] * t * damping
    acc[...] = jnp.zeros((NA, TILE, TILE), F32)

    def add(k, a, b):
        acc[a] += kbuf[k] * weight[pl.ds(b, 1)]

    each_tile(list_ref, add)
    for a in range(NA):
        row = cost_ref[a : a + 1] + row_form(acc[a])
        for d in range(16):
            send_ref[d, a : a + 1] = row


def push_kernel(
    list_ref, recv_ref, sum_ref, alpha_ref, cost_ref, kbuf, _,
    send_ref, s_ref,
    col, acc,
):
    s = jnp.where(live_rows(list_ref), -total(recv_ref, 0, NA) / sum_ref[...], 0.0)
    s_ref[...] = s
    weight = alpha_ref[...] * s * damping
    for a in range(NA):
        col[a] = column_form(weight[a : a + 1])
    acc[...] = jnp.zeros((NB, 8, TILE), F32)

    def add(k, a, b):
        acc[b] += fold(kbuf[k] * col[a])

    each_tile(list_ref, add)
    write_copies(send_ref, NB, cost_ref[...] + jnp.sum(acc[...], axis=1))


def gradient_kernel(
    list_ref, recv_ref, sum_ref, beta_ref, alpha_ref, s_ref, u_ref, v_ref,
    own_cells, c1, c2, c3, t0, t1, t2, t3, xbuf,
    g_ref, source_ref, target_ref,
    tbuf, cells_ref, col, col2, trow, vrow, prod, sem,
):
    pulls = pulls_of(own_cells, (c1, c2, c3), (t0, t1, t2, t3), cells_ref, tbuf, sem)
    for pull in pulls:
        pull.start()
    part = part_index()
    own = pl.ds(lax.axis_index("x") * 4 + lax.axis_index("zh"), 1)
    u = u_ref[...] + jnp.log(alpha_ref[...])
    vrow[...] = v_ref[...] + jnp.log(beta_ref[...])
    source_ref[...] = entropy * (u_ref[own] + jnp.log(alpha_ref[own]))
    own = pl.ds(pl.multiple_of(part * TB_DEV, TB_DEV), TB_DEV)
    target_ref[...] = entropy * vrow[own]
    trow[...] = -total(recv_ref, 0, NB) / sum_ref[...]
    for a in range(NA):
        col[a] = column_form(u[a : a + 1])
        col2[a] = column_form(1.0 + s_ref[a : a + 1])
    prod[...] = jnp.zeros((NA, TILE, D), F32)
    for pull in pulls:
        pull.wait()

    def add(k, a, b):
        slot = jnp.bitwise_xor(lax.shift_right_logical(b, 3), part)
        rows = pl.ds(pl.multiple_of(jnp.bitwise_and(b, TB_DEV - 1) * TILE, TILE), TILE)
        x = xbuf[k]
        weights = jnp.exp(x + col[a] + vrow[pl.ds(b, 1)]) * (x + col2[a] + trow[pl.ds(b, 1)])
        prod[a] += jnp.dot(
            weights.astype(jnp.bfloat16), tbuf[slot, rows, :], preferred_element_type=F32
        )

    each_tile(list_ref, add)
    contract = (((0,), (0,)), ((), ()))

    def outer(a, so_far):
        value = prod[a]
        high = value.astype(jnp.bfloat16)
        rest = value - high.astype(F32)
        middle = rest.astype(jnp.bfloat16)
        low = (rest - middle.astype(F32)).astype(jnp.bfloat16)
        cells = cells_ref[a]
        for piece in (low, middle, high):
            so_far = so_far + lax.dot_general(cells, piece, contract, preferred_element_type=F32)
        return so_far

    g = lax.fori_loop(0, NA, outer, jnp.zeros((D, D), F32))
    g_ref[...] = g * (-1.0 / math.sqrt(D))


def swap(value, axis):
    return lax.ppermute(value, axis, [(0, 1), (1, 0)])


def shifted(value, axis):
    return [lax.ppermute(value, axis, [(i, (i + k) % 4) for i in range(4)]) for k in (1, 2, 3)]


def row_exchange(value):
    return lax.all_to_all(value, ROW, 0, 0)


def col_exchange(value):
    return lax.all_to_all(value, COL, 0, 0)


def shards(
    source_cells,
    target_cells,
    mapping,
    source_logmass,
    target_logmass,
    group_blocks,
    tile_source,
    tile_target,
):
    codes = jnp.where(tile_source >= 0, tile_source * TB_DEV + tile_target, -1)
    codes0 = jnp.concatenate([codes, group_blocks.reshape(1, 4)], axis=1)
    first = (
        swap(codes0, "zl"),
        swap(codes0, "core"),
        *shifted(source_cells, "zh"),
        swap(target_cells, "zl"),
        swap(target_cells, "core"),
        source_logmass.astype(F32).reshape(1, TILE),
        target_logmass.astype(F32).reshape(TB_DEV, TILE),
    )
    codes2, codes1, z1, z2, z3, t2, t1, own_mass, own_target_mass = lax.optimization_barrier(first)
    codes3 = swap(codes2, "core")
    own_cells = jnp.stack([source_cells, z1, z2, z3])
    cells = (own_cells, *shifted(own_cells, "x"))
    targets = (target_cells, t1, t2, swap(t2, "core"))

    rows_to = (VM, SHAPE((16, NA, TILE), F32))
    cols_to = (VM, SHAPE((16, NB, TILE), F32))
    rows_state = (VM, SHAPE((NA, TILE), F32))
    cols_state = (VM, SHAPE((NB, TILE), F32))
    tiles = (HERE, SHAPE((SLOTS, TILE, TILE), F32))
    row_blocks = pltpu.VMEM((NA, TILE, TILE), F32)
    col_rows = pltpu.VMEM((NB, 8, TILE), F32)
    gathered = [
        pltpu.VMEM((4, TB_DEV * TILE, D), jnp.bfloat16),
        pltpu.VMEM((NA, TILE, D), jnp.bfloat16),
    ]
    gathered_sems = pltpu.SemaphoreType.DMA((21,))
    gathered_refs = [(ANY, value) for value in cells] + [(FAR, targets[0])] + [(ANY, value) for value in targets[1:]]

    send, tile_list, x = call(
        scores_kernel,
        "scores",
        [
            (SM, codes0), (SM, codes1), (SM, codes2), (SM, codes3), *gathered_refs,
            (FAR, mapping), (VM, own_mass),
        ],
        [(VM, SHAPE((16, NA + 8, TILE), F32)), (SM, SHAPE((SLOTS + 8,), jnp.int32)), tiles],
        [
            *gathered, pltpu.VMEM((D, D), jnp.bfloat16), pltpu.VMEM((NA, TILE, D), jnp.bfloat16),
            row_blocks, row_blocks, gathered_sems,
        ],
    )
    tile_list, x = (SM, tile_list), (HERE, x)
    recv = row_exchange(send)
    send, u, source_mass = call(
        first_targets_kernel,
        "first_targets",
        [tile_list, (VM, recv), x, (VM, own_target_mass)],
        [(VM, SHAPE((16, NB + TB_DEV, TILE), F32)), rows_state, rows_state],
        [row_blocks, col_rows, col_rows],
    )
    recv = col_exchange(send)
    send, v, target_mass, k = call(
        kernel_matrix_kernel,
        "kernel_matrix",
        [tile_list, (VM, recv), (VM, u), x],
        [rows_to, cols_state, cols_state, tiles],
        [row_blocks, row_blocks],
    )
    k = (HERE, k)
    for sweep in range(1, SINK):
        recv = row_exchange(send)
        send, alpha = call(
            columns_kernel,
            "columns",
            [tile_list, (VM, recv), (VM, source_mass), k, x],
            [cols_to, rows_state],
            [row_blocks, col_rows],
        )
        recv = col_exchange(send)
        if sweep < SINK - 1:
            send, _ = call(
                rows_kernel,
                "rows",
                [tile_list, (VM, recv), (VM, target_mass), k, x],
                [rows_to, cols_state],
                [row_blocks],
            )
    send, beta, column_sum, row_cost = call(
        masses_kernel,
        "masses",
        [tile_list, (VM, recv), (VM, target_mass), k, x],
        [(VM, SHAPE((16, 2 * NA, TILE), F32)), cols_state, cols_state, rows_state],
        [row_blocks, row_blocks],
    )
    recv = row_exchange(send)
    send, row_sum, s, column_cost = call(
        first_ratio_kernel,
        "first_ratio",
        [tile_list, (VM, recv), (VM, alpha), k, x],
        [cols_to, rows_state, rows_state, cols_state],
        [row_blocks, row_blocks, col_rows, col_rows],
    )
    recv = col_exchange(send)
    for _ in range(1, ADJ):
        (send,) = call(
            pull_kernel,
            "pull",
            [tile_list, (VM, recv), (VM, column_sum), (VM, beta), (VM, row_cost), k, x],
            [rows_to],
            [row_blocks, pltpu.VMEM((NB, TILE), F32)],
        )
        recv = row_exchange(send)
        send, s = call(
            push_kernel,
            "push",
            [tile_list, (VM, recv), (VM, row_sum), (VM, alpha), (VM, column_cost), k, x],
            [cols_to, rows_state],
            [row_blocks, col_rows],
        )
        recv = col_exchange(send)
    gradient, own_source, own_target = call(
        gradient_kernel,
        "gradient",
        [
            tile_list, (VM, recv), (VM, column_sum), (VM, beta), (VM, alpha), (VM, s), (VM, u), (VM, v),
            *gathered_refs, x,
        ],
        [(VM, SHAPE((D, D), F32)), (VM, SHAPE((1, TILE), F32)), (VM, SHAPE((TB_DEV, TILE), F32))],
        [
            *gathered, row_blocks, row_blocks, pltpu.VMEM((NB, TILE), F32), pltpu.VMEM((NB, TILE), F32),
            pltpu.VMEM((NA, TILE, D), F32), gathered_sems,
        ],
    )
    piece = jnp.sum(col_exchange(gradient.reshape(16, 16, D)), axis=0)
    piece = jnp.sum(row_exchange(jnp.broadcast_to(piece[None], (16, 16, D))), axis=0)
    map_gradient = col_exchange(jnp.broadcast_to(piece[None], (16, 16, D))).reshape(D, D)

    return (own_source.reshape(TILE), own_target.reshape(TB_DEV * TILE), map_gradient)


def solution(mesh):
    grid = Mesh(mesh.devices.reshape(4, 4, 4, 2, 2), AXES)
    tgt = ("x", "zh", "zl", "core")
    both = ("src", *tgt)
    in_specs = (
        P(both, None),
        P(tgt, None),
        P(),
        P(both),
        P(tgt),
        P(),
        P(both, None),
        P(both, None),
    )
    out_specs = (P(both), P(tgt), P())
    return jax.shard_map(shards, mesh=grid, in_specs=in_specs, out_specs=out_specs, check_vma=False)
```

```python
import math

import jax
import jax.numpy as jnp
from jax import lax
from jax.experimental import pallas as pl
from jax.experimental.pallas import tpu as pltpu
from jax.sharding import Mesh, PartitionSpec as P

TILE = 128
TB_DEV = 8
TILES = 64
SINK = 4
ADJ = 4
D = 256

entropy = 0.5
damping = 0.8
lowest = -1e30

AXES = ("src", "x", "zh", "zl", "core")
ROW = ("x", "zh")
COL = ("src", "zl", "core")
NA = 16
NB = 32
SLOTS = 4 * TILES
CHUNK = 8
F32 = jnp.float32


VM = pl.BlockSpec(memory_space=pltpu.VMEM)
SM = pl.BlockSpec(memory_space=pltpu.SMEM)
ANY = pl.BlockSpec(memory_space=pl.ANY)
SHAPE = jax.ShapeDtypeStruct


HERE = "here"
FAR = "far"


def call(kernel, name, ins, outs, scratch, flops=2 << 20, moved=1 << 20, vmem=9, aliases={}):
    in_specs, args = [], []
    for spec, value in ins:
        if spec in (HERE, FAR):
            space = pltpu.VMEM if spec == HERE else pltpu.HBM
            spec, value = pl.BlockSpec(memory_space=space), pltpu.with_memory_space_constraint(value, space)
        in_specs.append(spec)
        args.append(value)
    outs = [(VM, pltpu.VMEM(shape.shape, shape.dtype)) if spec == HERE else (spec, shape) for spec, shape in outs]
    return pl.pallas_call(
        kernel,
        out_shape=[shape for _, shape in outs],
        in_specs=in_specs,
        out_specs=[spec for spec, _ in outs],
        scratch_shapes=scratch,
        input_output_aliases=aliases,
        name=name,
        cost_estimate=pl.CostEstimate(flops=flops, bytes_accessed=moved, transcendentals=0),
        compiler_params=pltpu.CompilerParams(vmem_limit_bytes=vmem << 20),
    )(*args)


def row_form(block):
    return jnp.sum(block.T, axis=0, keepdims=True)


def column_form(row):
    return jnp.broadcast_to(row, (TILE, TILE)).T


def fold(block):
    return jnp.sum(block.reshape(16, 8, TILE), axis=0)


def fold_max(block):
    return jnp.max(block.reshape(16, 8, TILE), axis=0)


def each_tile(list_ref, body):
    def one(c, carry):
        for step in range(CHUNK):
            k = c * CHUNK + step
            code = list_ref[k]
            body(k, lax.shift_right_logical(code, 5), jnp.bitwise_and(code, NB - 1))
        return carry

    lax.fori_loop(0, lax.shift_right_logical(list_ref[SLOTS] + (CHUNK - 1), 3), one, 0)


def each_chunk(list_ref, bodies):
    def one(c, carry):
        codes = [list_ref[c * CHUNK + step] for step in range(CHUNK)]
        for body in bodies:
            for step, code in enumerate(codes):
                body(step, c * CHUNK + step, lax.shift_right_logical(code, 5), jnp.bitwise_and(code, NB - 1))
        return carry

    lax.fori_loop(0, lax.shift_right_logical(list_ref[SLOTS] + (CHUNK - 1), 3), one, 0)


def part_index():
    return lax.axis_index("zl") * 2 + lax.axis_index("core")


def pulls_of(cells_far, targets, cells, tbuf, sem):
    pulls = [pltpu.make_async_copy(target, tbuf.at[r], sem.at[r]) for r, target in enumerate(targets)]
    return [*pulls, pltpu.make_async_copy(cells_far, cells, sem.at[4])]


def write_copies(out_ref, rows, value, first=0):
    for d in range(16):
        out_ref[d, first : first + rows] = value


def live_rows(list_ref):
    block = 4 * lax.broadcasted_iota(jnp.int32, (NA, TILE), 0) + part_index()
    return block < list_ref[SLOTS + 1]


def total(recv_ref, first, rows):
    so_far = recv_ref[0, first : first + rows]
    for d in range(1, 16):
        so_far = so_far + recv_ref[d, first : first + rows]
    return so_far


def merged(recv_ref, rows):
    largest = recv_ref[0, 0:rows]
    for d in range(1, 16):
        largest = jnp.maximum(largest, recv_ref[d, 0:rows])
    so_far = jnp.zeros((rows, TILE), F32)
    for d in range(16):
        so_far = so_far + jnp.exp(recv_ref[d, 0:rows] - largest)
    return largest + jnp.log(so_far)


def finish_log(largest, so_far):
    good = so_far > 0
    return jnp.where(good, largest + jnp.log(jnp.where(good, so_far, 1.0)), lowest)


def plan_kernel(notes0, notes1, notes2, notes3, list_ref):
    part = part_index()
    count = 0
    for r, notes in enumerate((notes0, notes1, notes2, notes3)):
        base = jnp.bitwise_xor(part, r) * TB_DEV

        def gather(k, n, notes=notes, base=base):
            code = notes[0, k].astype(jnp.int32)
            source = lax.shift_right_arithmetic(code, 3)
            take = jnp.logical_and(code >= 0, jnp.bitwise_and(source, 3) == part)
            target = base + jnp.bitwise_and(code, TB_DEV - 1)
            list_ref[n] = lax.shift_right_arithmetic(source, 2) * NB + target
            return n + take.astype(jnp.int32)

        count = lax.fori_loop(0, TILES, gather, count, unroll=8)

    def clear(k, carry):
        list_ref[k] = 0
        return carry

    lax.fori_loop(count, jnp.minimum(count + CHUNK, SLOTS), clear, 0)
    list_ref[SLOTS] = count
    list_ref[SLOTS + 1] = notes0[0, TILES + lax.axis_index("src")].astype(jnp.int32)


def scores_kernel(
    list_ref, cells_far, t0, t1, t2, t3, mapping_far, mass_ref,
    send_ref, xbuf, _,
    tbuf, cells_ref, mapping_ref, mapped, top, acc, sem,
):
    pulls = pulls_of(cells_far, (t0, t1, t2, t3), cells_ref, tbuf, sem)
    pulls.append(pltpu.make_async_copy(mapping_far, mapping_ref, sem.at[5]))
    for pull in pulls:
        pull.start()
    part = part_index()
    count = list_ref[SLOTS]
    for pull in pulls:
        pull.wait()

    def blank(a, carry):
        top[a] = jnp.full((TILE, TILE), lowest, F32)
        acc[a] = jnp.zeros((TILE, TILE), F32)
        product = jnp.dot(cells_ref[a], mapping_ref[...], preferred_element_type=F32)
        mapped[a] = product.astype(jnp.bfloat16)
        return carry

    lax.fori_loop(0, NA, blank, 0)
    scale = (1.0 / entropy) / math.sqrt(D)

    def product(step, k, a, b):
        slot = jnp.bitwise_xor(lax.shift_right_logical(b, 3), part)
        rows = pl.ds(pl.multiple_of(jnp.bitwise_and(b, TB_DEV - 1) * TILE, TILE), TILE)
        x = lax.dot_general(
            mapped[a], tbuf[slot, rows, :], (((1,), (1,)), ((), ())), preferred_element_type=F32
        )
        xbuf[k] = jnp.where(k < count, x * scale, lowest)

    def largest(step, k, a, b):
        top[a] = jnp.maximum(top[a], xbuf[k])

    each_chunk(list_ref, (product, largest))

    def spread(a, carry):
        top[a] = jnp.broadcast_to(jnp.max(top[a], axis=1, keepdims=True), (TILE, TILE))
        return carry

    lax.fori_loop(0, NA, spread, 0)

    def add(k, a, b):
        acc[a] += jnp.exp(xbuf[k] - top[a])

    each_tile(list_ref, add)
    for a in range(NA):
        row = finish_log(top[a].T[0:1], row_form(acc[a]))
        for d in range(16):
            send_ref[d, a : a + 1] = row
    write_copies(send_ref, 8, jnp.broadcast_to(mass_ref[...], (8, TILE)), NA)


def first_targets_kernel(
    list_ref, recv_ref, xbuf, _,
    send_ref, u_ref, mass_out,
    col, top, acc,
):
    for a in range(NA):
        mass_out[a : a + 1] = recv_ref[a, NA : NA + 1]
    u = jnp.where(live_rows(list_ref), mass_out[...] - merged(recv_ref, NA), 0.0)
    u_ref[...] = u
    for a in range(NA):
        col[a] = column_form(u[a : a + 1])
    top[...] = jnp.full((NB, 8, TILE), lowest, F32)
    acc[...] = jnp.zeros((NB, 8, TILE), F32)

    def largest(k, a, b):
        top[b] = jnp.maximum(top[b], fold_max(xbuf[k] + col[a]))

    each_tile(list_ref, largest)
    for b in range(NB):
        top[b] = jnp.broadcast_to(jnp.max(top[b], axis=0, keepdims=True), (8, TILE))

    def add(k, a, b):
        acc[b] += fold(jnp.exp(xbuf[k] + col[a] - top[b][0:1]))

    each_tile(list_ref, add)
    for b in range(NB):
        row = finish_log(top[b][0:1], jnp.sum(acc[b], axis=0, keepdims=True))
        for d in range(16):
            send_ref[d, b : b + 1] = row


def kernel_matrix_kernel(
    list_ref, recv_ref, u_ref, notes0, notes1, notes2, notes3, xbuf, _,
    send_ref, v_ref, mass_out, kbuf,
    col, acc,
):
    for r, notes in enumerate((notes0, notes1, notes2, notes3)):
        first = pl.multiple_of(jnp.bitwise_xor(part_index(), r) * TB_DEV, TB_DEV)
        mass_out[pl.ds(first, TB_DEV)] = notes[TB_DEV : 2 * TB_DEV]
    v_ref[...] = mass_out[...] - merged(recv_ref, NB)
    for a in range(NA):
        col[a] = column_form(u_ref[a : a + 1])
    acc[...] = jnp.zeros((NA, TILE, TILE), F32)

    def build(k, a, b):
        value = jnp.exp(xbuf[k] + col[a] + v_ref[pl.ds(b, 1)])
        kbuf[k] = value
        acc[a] += value

    each_tile(list_ref, build)
    for a in range(NA):
        row = row_form(acc[a])
        for d in range(16):
            send_ref[d, a : a + 1] = row


def columns_kernel(list_ref, recv_ref, mass_ref, kbuf, _, send_ref, *rest):
    *kept, col, acc = rest
    alpha = jnp.where(live_rows(list_ref), jnp.exp(mass_ref[...]) / total(recv_ref, 0, NA), 1.0)
    for ref in kept:
        ref[...] = alpha
    for a in range(NA):
        col[a] = column_form(alpha[a : a + 1])
    acc[...] = jnp.zeros((NB, 8, TILE), F32)

    def add(k, a, b):
        acc[b] += fold(kbuf[k] * col[a])

    each_tile(list_ref, add)
    write_copies(send_ref, NB, jnp.sum(acc[...], axis=1))


def rows_kernel(list_ref, recv_ref, mass_ref, kbuf, _, send_ref, beta_ref, acc):
    beta_ref[...] = jnp.exp(mass_ref[...]) / total(recv_ref, 0, NB)
    acc[...] = jnp.zeros((NA, TILE, TILE), F32)

    def add(k, a, b):
        acc[a] += kbuf[k] * beta_ref[pl.ds(b, 1)]

    each_tile(list_ref, add)
    for a in range(NA):
        row = row_form(acc[a])
        for d in range(16):
            send_ref[d, a : a + 1] = row


def masses_kernel(
    list_ref, recv_ref, mass_ref, kbuf, xbuf,
    send_ref, beta_ref, sum_ref, cost_ref,
    acc, acc_cost,
):
    column_sum = total(recv_ref, 0, NB)
    sum_ref[...] = column_sum
    beta_ref[...] = jnp.exp(mass_ref[...]) / column_sum
    acc[...] = jnp.zeros((NA, TILE, TILE), F32)
    acc_cost[...] = jnp.zeros((NA, TILE, TILE), F32)

    def add(k, a, b):
        plan = kbuf[k] * beta_ref[pl.ds(b, 1)]
        acc[a] += plan
        acc_cost[a] += plan * xbuf[k]

    each_tile(list_ref, add)
    for a in range(NA):
        row = row_form(acc[a])
        cost = row_form(acc_cost[a])
        cost_ref[a : a + 1] = cost
        for d in range(16):
            send_ref[d, a : a + 1] = row
            send_ref[d, NA + a : NA + a + 1] = cost


def first_ratio_kernel(
    list_ref, recv_ref, alpha_ref, kbuf, xbuf,
    send_ref, sum_ref, cost_ref,
    col, col2, acc, acc2,
):
    row_sum = total(recv_ref, 0, NA)
    sum_ref[...] = row_sum
    s = jnp.where(live_rows(list_ref), -total(recv_ref, NA, NA) / row_sum, 0.0)
    for a in range(NA):
        col[a] = column_form(alpha_ref[a : a + 1])
        col2[a] = column_form(s[a : a + 1] * damping)
    acc[...] = jnp.zeros((NB, 8, TILE), F32)
    acc2[...] = jnp.zeros((NB, 8, TILE), F32)

    def add(k, a, b):
        plan = kbuf[k] * col[a]
        acc[b] += fold(plan * xbuf[k])
        acc2[b] += fold(plan * (xbuf[k] + col2[a]))

    each_tile(list_ref, add)
    cost_ref[...] = jnp.sum(acc[...], axis=1)
    write_copies(send_ref, NB, jnp.sum(acc2[...], axis=1))


def pull_kernel(
    list_ref, recv_ref, sum_ref, beta_ref, cost_ref, kbuf, _,
    send_ref,
    acc, weight,
):
    t = -total(recv_ref, 0, NB) / sum_ref[...]
    weight[...] = beta_ref[...] * t * damping
    acc[...] = jnp.zeros((NA, TILE, TILE), F32)

    def add(k, a, b):
        acc[a] += kbuf[k] * weight[pl.ds(b, 1)]

    each_tile(list_ref, add)
    for a in range(NA):
        row = cost_ref[a : a + 1] + row_form(acc[a])
        for d in range(16):
            send_ref[d, a : a + 1] = row


def push_kernel(
    list_ref, recv_ref, sum_ref, alpha_ref, cost_ref, kbuf, _,
    send_ref, *rest,
):
    *kept, col, acc = rest
    s = jnp.where(live_rows(list_ref), -total(recv_ref, 0, NA) / sum_ref[...], 0.0)
    for ref in kept:
        ref[...] = s
    weight = alpha_ref[...] * s * damping
    for a in range(NA):
        col[a] = column_form(weight[a : a + 1])
    acc[...] = jnp.zeros((NB, 8, TILE), F32)

    def add(k, a, b):
        acc[b] += fold(kbuf[k] * col[a])

    each_tile(list_ref, add)
    write_copies(send_ref, NB, cost_ref[...] + jnp.sum(acc[...], axis=1))


def gradient_kernel(
    list_ref, recv_ref, sum_ref, beta_ref, alpha_ref, s_ref, u_ref, v_ref,
    cells_far, t0, t1, t2, t3, xbuf,
    g_ref, source_ref, target_ref,
    tbuf, cells_ref, col, col2, trow, vrow, prod, wbuf, pbuf, sem,
):
    pulls = pulls_of(cells_far, (t0, t1, t2, t3), cells_ref, tbuf, sem)
    for pull in pulls:
        pull.start()
    part = part_index()
    own = pl.ds(lax.axis_index("x") * 4 + lax.axis_index("zh"), 1)
    u = u_ref[...] + jnp.log(alpha_ref[...])
    vrow[...] = v_ref[...] + jnp.log(beta_ref[...])
    source_ref[...] = entropy * (u_ref[own] + jnp.log(alpha_ref[own]))
    own = pl.ds(pl.multiple_of(part * TB_DEV, TB_DEV), TB_DEV)
    target_ref[...] = entropy * vrow[own]
    trow[...] = -total(recv_ref, 0, NB) / sum_ref[...]
    for a in range(NA):
        col[a] = column_form(u[a : a + 1])
        col2[a] = column_form(1.0 + s_ref[a : a + 1])
    prod[...] = jnp.zeros((NA, TILE, D), F32)
    for pull in pulls:
        pull.wait()

    def weigh(step, k, a, b):
        x = xbuf[k]
        weights = jnp.exp(x + col[a] + vrow[pl.ds(b, 1)]) * (x + col2[a] + trow[pl.ds(b, 1)])
        wbuf[step] = weights.astype(jnp.bfloat16)

    def multiply(step, k, a, b):
        slot = jnp.bitwise_xor(lax.shift_right_logical(b, 3), part)
        rows = pl.ds(pl.multiple_of(jnp.bitwise_and(b, TB_DEV - 1) * TILE, TILE), TILE)
        pbuf[step] = jnp.dot(wbuf[step], tbuf[slot, rows, :], preferred_element_type=F32)

    def add(step, k, a, b):
        prod[a] += pbuf[step]

    each_chunk(list_ref, (weigh, multiply, add))
    contract = (((0,), (0,)), ((), ()))

    def outer(a, so_far):
        value = prod[a]
        high = value.astype(jnp.bfloat16)
        rest = value - high.astype(F32)
        middle = rest.astype(jnp.bfloat16)
        low = (rest - middle.astype(F32)).astype(jnp.bfloat16)
        cells = cells_ref[a]
        for piece in (low, middle, high):
            so_far = so_far + lax.dot_general(cells, piece, contract, preferred_element_type=F32)
        return so_far

    g = lax.fori_loop(0, NA, outer, jnp.zeros((D, D), F32))
    g_ref[...] = g * (-1.0 / math.sqrt(D))


def swap(value, axis):
    return lax.ppermute(value, axis, [(0, 1), (1, 0)])


def row_exchange(value):
    return lax.all_to_all(value, ROW, 0, 0)


def col_exchange(value):
    return lax.all_to_all(value, COL, 0, 0)


def shards(
    source_cells,
    target_cells,
    mapping,
    source_logmass,
    target_logmass,
    group_blocks,
    tile_source,
    tile_target,
):
    codes = jnp.where(tile_source >= 0, tile_source * TB_DEV + tile_target, -1)
    head = jnp.concatenate([codes, group_blocks.reshape(1, 4)], axis=1).astype(F32)
    note = jnp.concatenate(
        [jnp.pad(head, ((0, 7), (0, TILE - TILES - 4))), target_logmass.astype(F32).reshape(TB_DEV, TILE)]
    )
    first = (
        lax.all_to_all(jnp.broadcast_to(source_cells[None], (4, TILE, D)), "zh", 0, 0),
        swap(note, "zl"),
        swap(note, "core"),
        swap(target_cells, "core"),
        source_logmass.astype(F32).reshape(1, TILE),
        target_cells,
    )
    column_cells, note2, note1, t1, own_mass, t0 = lax.optimization_barrier(first)
    t2 = swap(t0, "zl")
    notes = (note, note1, note2, swap(note2, "core"))
    targets = (target_cells, t1, t2, swap(t2, "core"))
    cells = lax.all_to_all(jnp.broadcast_to(column_cells[None], (4, 4, TILE, D)), "x", 0, 0)
    cells = cells.reshape(NA, TILE, D)

    rows_to = (VM, SHAPE((16, NA, TILE), F32))
    cols_to = (VM, SHAPE((16, NB, TILE), F32))
    rows_state = (VM, SHAPE((NA, TILE), F32))
    cols_state = (VM, SHAPE((NB, TILE), F32))
    tiles = (HERE, SHAPE((SLOTS, TILE, TILE), F32))
    row_blocks = pltpu.VMEM((NA, TILE, TILE), F32)
    col_rows = pltpu.VMEM((NB, 8, TILE), F32)
    gathered = [
        pltpu.VMEM((4, TB_DEV * TILE, D), jnp.bfloat16),
        pltpu.VMEM((NA, TILE, D), jnp.bfloat16),
    ]
    gathered_sems = pltpu.SemaphoreType.DMA((6,))
    gathered_refs = [(ANY, cells), (FAR, targets[0]), *[(ANY, value) for value in targets[1:]]]

    (tile_list,) = call(
        plan_kernel,
        "plan",
        [(SM, note) for note in notes],
        [(SM, SHAPE((SLOTS + 8,), jnp.int32))],
        [],
    )
    send, x, k = call(
        scores_kernel,
        "scores",
        [
            (SM, tile_list), *gathered_refs,
            (FAR, mapping), (VM, own_mass),
        ],
        [(VM, SHAPE((16, NA + 8, TILE), F32)), tiles, tiles],
        [
            *gathered, pltpu.VMEM((D, D), jnp.bfloat16), pltpu.VMEM((NA, TILE, D), jnp.bfloat16),
            row_blocks, row_blocks, gathered_sems,
        ],
    )
    tile_list, x = (SM, tile_list), (HERE, x)
    recv = row_exchange(send)
    send, u, source_mass = call(
        first_targets_kernel,
        "first_targets",
        [tile_list, (VM, recv), x, (HERE, k)],
        [cols_to, rows_state, rows_state],
        [row_blocks, col_rows, col_rows],
    )
    recv = col_exchange(send)
    send, v, target_mass, k = call(
        kernel_matrix_kernel,
        "kernel_matrix",
        [tile_list, (VM, recv), (VM, u), *[(VM, note) for note in notes], x, (HERE, k)],
        [rows_to, cols_state, cols_state, tiles],
        [row_blocks, row_blocks],
        aliases={8: 3},
    )
    k = (HERE, k)
    for sweep in range(1, SINK):
        recv = row_exchange(send)
        send, *kept = call(
            columns_kernel,
            "columns",
            [tile_list, (VM, recv), (VM, source_mass), k, x],
            [cols_to, *([rows_state] if sweep == SINK - 1 else [])],
            [row_blocks, col_rows],
        )
        recv = col_exchange(send)
        if sweep < SINK - 1:
            (send,) = call(
                rows_kernel,
                "rows",
                [tile_list, (VM, recv), (VM, target_mass), k, x],
                [rows_to],
                [pltpu.VMEM((NB, TILE), F32), row_blocks],
            )
    (alpha,) = kept
    send, beta, column_sum, row_cost = call(
        masses_kernel,
        "masses",
        [tile_list, (VM, recv), (VM, target_mass), k, x],
        [(VM, SHAPE((16, 2 * NA, TILE), F32)), cols_state, cols_state, rows_state],
        [row_blocks, row_blocks],
    )
    recv = row_exchange(send)
    send, row_sum, column_cost = call(
        first_ratio_kernel,
        "first_ratio",
        [tile_list, (VM, recv), (VM, alpha), k, x],
        [cols_to, rows_state, cols_state],
        [row_blocks, row_blocks, col_rows, col_rows],
    )
    recv = col_exchange(send)
    for step in range(1, ADJ):
        (send,) = call(
            pull_kernel,
            "pull",
            [tile_list, (VM, recv), (VM, column_sum), (VM, beta), (VM, row_cost), k, x],
            [rows_to],
            [row_blocks, pltpu.VMEM((NB, TILE), F32)],
        )
        recv = row_exchange(send)
        send, *kept = call(
            push_kernel,
            "push",
            [tile_list, (VM, recv), (VM, row_sum), (VM, alpha), (VM, column_cost), k, x],
            [cols_to, *([rows_state] if step == ADJ - 1 else [])],
            [row_blocks, col_rows],
        )
        recv = col_exchange(send)
    (s,) = kept
    gradient, own_source, own_target = call(
        gradient_kernel,
        "gradient",
        [
            tile_list, (VM, recv), (VM, column_sum), (VM, beta), (VM, alpha), (VM, s), (VM, u), (VM, v),
            *gathered_refs, x,
        ],
        [(VM, SHAPE((D, D), F32)), (VM, SHAPE((1, TILE), F32)), (VM, SHAPE((TB_DEV, TILE), F32))],
        [
            *gathered, row_blocks, row_blocks, pltpu.VMEM((NB, TILE), F32), pltpu.VMEM((NB, TILE), F32),
            pltpu.VMEM((NA, TILE, D), F32),
            pltpu.VMEM((CHUNK, TILE, TILE), jnp.bfloat16), pltpu.VMEM((CHUNK, TILE, D), F32), gathered_sems,
        ],
    )
    piece = jnp.sum(col_exchange(gradient.reshape(16, 16, D)), axis=0)
    piece = jnp.sum(row_exchange(jnp.broadcast_to(piece[None], (16, 16, D))), axis=0)
    map_gradient = col_exchange(jnp.broadcast_to(piece[None], (16, 16, D))).reshape(D, D)

    return (own_source.reshape(TILE), own_target.reshape(TB_DEV * TILE), map_gradient)


def solution(mesh):
    grid = Mesh(mesh.devices.reshape(4, 4, 4, 2, 2), AXES)
    tgt = ("x", "zh", "zl", "core")
    both = ("src", *tgt)
    in_specs = (
        P(both, None),
        P(tgt, None),
        P(),
        P(both),
        P(tgt),
        P(),
        P(both, None),
        P(both, None),
    )
    out_specs = (P(both), P(tgt), P())
    return jax.shard_map(shards, mesh=grid, in_specs=in_specs, out_specs=out_specs, check_vma=False)
```

```python
import math

import jax
import jax.numpy as jnp
from jax import lax
from jax.experimental import pallas as pl
from jax.experimental.pallas import tpu as pltpu
from jax.sharding import Mesh, PartitionSpec as P

TILE = 128
TB_DEV = 8
TILES = 64
SINK = 4
ADJ = 4
D = 256

entropy = 0.5
damping = 0.8
lowest = -1e30

AXES = ("src", "x", "zh", "zl", "core")
ROW = ("x", "zh")
COL = ("src", "zl", "core")
NA = 16
NB = 32
SLOTS = 4 * TILES
CHUNK = 8
F32 = jnp.float32


VM = pl.BlockSpec(memory_space=pltpu.VMEM)
SM = pl.BlockSpec(memory_space=pltpu.SMEM)
ANY = pl.BlockSpec(memory_space=pl.ANY)
SHAPE = jax.ShapeDtypeStruct


HERE = "here"
FAR = "far"


def call(kernel, name, ins, outs, scratch, flops=2 << 20, moved=1 << 20, vmem=10, aliases={}):
    in_specs, args = [], []
    for spec, value in ins:
        if spec in (HERE, FAR):
            space = pltpu.VMEM if spec == HERE else pltpu.HBM
            spec, value = pl.BlockSpec(memory_space=space), pltpu.with_memory_space_constraint(value, space)
        in_specs.append(spec)
        args.append(value)
    outs = [(VM, pltpu.VMEM(shape.shape, shape.dtype)) if spec == HERE else (spec, shape) for spec, shape in outs]
    return pl.pallas_call(
        kernel,
        out_shape=[shape for _, shape in outs],
        in_specs=in_specs,
        out_specs=[spec for spec, _ in outs],
        scratch_shapes=scratch,
        input_output_aliases=aliases,
        name=name,
        cost_estimate=pl.CostEstimate(flops=flops, bytes_accessed=moved, transcendentals=0),
        compiler_params=pltpu.CompilerParams(vmem_limit_bytes=vmem << 20),
    )(*args)


def row_form(block):
    return jnp.sum(block.T, axis=0, keepdims=True)


def column_form(row):
    return jnp.broadcast_to(row, (TILE, TILE)).T


def fold(block):
    return jnp.sum(block.reshape(16, 8, TILE), axis=0)


def fold_max(block):
    return jnp.max(block.reshape(16, 8, TILE), axis=0)


def each_tile(list_ref, body):
    def one(c, carry):
        for step in range(CHUNK):
            k = c * CHUNK + step
            code = list_ref[k]
            body(k, lax.shift_right_logical(code, 5), jnp.bitwise_and(code, NB - 1))
        return carry

    lax.fori_loop(0, lax.shift_right_logical(list_ref[SLOTS] + (CHUNK - 1), 3), one, 0)


def each_chunk(list_ref, bodies):
    def one(c, carry):
        codes = [list_ref[c * CHUNK + step] for step in range(CHUNK)]
        for body in bodies:
            for step, code in enumerate(codes):
                body(step, c * CHUNK + step, lax.shift_right_logical(code, 5), jnp.bitwise_and(code, NB - 1))
        return carry

    lax.fori_loop(0, lax.shift_right_logical(list_ref[SLOTS] + (CHUNK - 1), 3), one, 0)


def part_index():
    return lax.axis_index("zl") * 2 + lax.axis_index("core")


def pulls_of(targets, tbuf, sem):
    return [pltpu.make_async_copy(target, tbuf.at[r], sem.at[r]) for r, target in enumerate(targets)]


def write_copies(out_ref, rows, value, first=0):
    for d in range(16):
        out_ref[d, first : first + rows] = value


def live_rows(list_ref):
    block = 4 * lax.broadcasted_iota(jnp.int32, (NA, TILE), 0) + part_index()
    return block < list_ref[SLOTS + 1]


def total(recv_ref, first, rows):
    so_far = recv_ref[0, first : first + rows]
    for d in range(1, 16):
        so_far = so_far + recv_ref[d, first : first + rows]
    return so_far


def merged(recv_ref, rows):
    largest = recv_ref[0, 0:rows]
    for d in range(1, 16):
        largest = jnp.maximum(largest, recv_ref[d, 0:rows])
    so_far = jnp.zeros((rows, TILE), F32)
    for d in range(16):
        so_far = so_far + jnp.exp(recv_ref[d, 0:rows] - largest)
    return largest + jnp.log(so_far)


def finish_log(largest, so_far):
    good = so_far > 0
    return jnp.where(good, largest + jnp.log(jnp.where(good, so_far, 1.0)), lowest)


def plan_kernel(notes0, notes1, notes2, notes3, list_ref):
    part = part_index()
    count = 0
    for r, notes in enumerate((notes0, notes1, notes2, notes3)):
        base = jnp.bitwise_xor(part, r) * TB_DEV

        def gather(k, n, notes=notes, base=base):
            code = notes[0, k].astype(jnp.int32)
            source = lax.shift_right_arithmetic(code, 3)
            take = jnp.logical_and(code >= 0, jnp.bitwise_and(source, 3) == part)
            target = base + jnp.bitwise_and(code, TB_DEV - 1)
            list_ref[n] = lax.shift_right_arithmetic(source, 2) * NB + target
            return n + take.astype(jnp.int32)

        count = lax.fori_loop(0, TILES, gather, count, unroll=8)

    def clear(k, carry):
        list_ref[k] = 0
        return carry

    lax.fori_loop(count, jnp.minimum(count + CHUNK, SLOTS), clear, 0)
    list_ref[SLOTS] = count
    list_ref[SLOTS + 1] = notes0[0, TILES + lax.axis_index("src")].astype(jnp.int32)


def scores_kernel(
    list_ref, cells_ref, t0, t1, t2, t3, mapping_far, mass_ref,
    send_ref, xbuf, _,
    tbuf, mapping_ref, mapped, top, acc, sem,
):
    pull_mapping = pltpu.make_async_copy(mapping_far, mapping_ref, sem.at[4])
    pull_mapping.start()
    pulls = pulls_of((t0, t1, t2, t3), tbuf, sem)
    for pull in pulls:
        pull.start()
    part = part_index()
    count = list_ref[SLOTS]
    top[...] = jnp.full((NA, TILE, TILE), lowest, F32)
    acc[...] = jnp.zeros((NA, TILE, TILE), F32)
    pull_mapping.wait()

    def embed(step, carry):
        rows = pl.ds(pl.multiple_of(step * 2 * D, 2 * D), 2 * D)
        product = jnp.dot(cells_ref[rows], mapping_ref[...], preferred_element_type=F32)
        mapped[rows] = product.astype(jnp.bfloat16)
        return carry

    lax.fori_loop(0, NA * TILE // (2 * D), embed, 0)
    for pull in pulls:
        pull.wait()
    scale = (1.0 / entropy) / math.sqrt(D)

    def product(step, k, a, b):
        slot = jnp.bitwise_xor(lax.shift_right_logical(b, 3), part)
        rows = pl.ds(pl.multiple_of(jnp.bitwise_and(b, TB_DEV - 1) * TILE, TILE), TILE)
        x = lax.dot_general(
            mapped[pl.ds(pl.multiple_of(a * TILE, TILE), TILE)], tbuf[slot, rows, :], (((1,), (1,)), ((), ())), preferred_element_type=F32
        )
        xbuf[k] = jnp.where(k < count, x * scale, lowest)

    def largest(step, k, a, b):
        top[a] = jnp.maximum(top[a], xbuf[k])

    each_chunk(list_ref, (product, largest))

    def spread(a, carry):
        top[a] = jnp.broadcast_to(jnp.max(top[a], axis=1, keepdims=True), (TILE, TILE))
        return carry

    lax.fori_loop(0, NA, spread, 0)

    def add(k, a, b):
        acc[a] += jnp.exp(xbuf[k] - top[a])

    each_tile(list_ref, add)
    for a in range(NA):
        row = finish_log(top[a].T[0:1], row_form(acc[a]))
        for d in range(16):
            send_ref[d, a : a + 1] = row
    write_copies(send_ref, 8, jnp.broadcast_to(mass_ref[...], (8, TILE)), NA)


def first_targets_kernel(
    list_ref, recv_ref, xbuf, _,
    send_ref, u_ref, mass_out,
    col, top, acc,
):
    for a in range(NA):
        mass_out[a : a + 1] = recv_ref[a, NA : NA + 1]
    u = jnp.where(live_rows(list_ref), mass_out[...] - merged(recv_ref, NA), 0.0)
    u_ref[...] = u
    for a in range(NA):
        col[a] = column_form(u[a : a + 1])
    top[...] = jnp.full((NB, 8, TILE), lowest, F32)
    acc[...] = jnp.zeros((NB, 8, TILE), F32)

    def largest(k, a, b):
        top[b] = jnp.maximum(top[b], fold_max(xbuf[k] + col[a]))

    each_tile(list_ref, largest)
    for b in range(NB):
        top[b] = jnp.broadcast_to(jnp.max(top[b], axis=0, keepdims=True), (8, TILE))

    def add(k, a, b):
        acc[b] += fold(jnp.exp(xbuf[k] + col[a] - top[b][0:1]))

    each_tile(list_ref, add)
    for b in range(NB):
        row = finish_log(top[b][0:1], jnp.sum(acc[b], axis=0, keepdims=True))
        for d in range(16):
            send_ref[d, b : b + 1] = row


def kernel_matrix_kernel(
    list_ref, recv_ref, u_ref, notes0, notes1, notes2, notes3, xbuf, _,
    send_ref, v_ref, mass_out, kbuf,
    col, acc,
):
    for r, notes in enumerate((notes0, notes1, notes2, notes3)):
        first = pl.multiple_of(jnp.bitwise_xor(part_index(), r) * TB_DEV, TB_DEV)
        mass_out[pl.ds(first, TB_DEV)] = notes[TB_DEV : 2 * TB_DEV]
    v_ref[...] = mass_out[...] - merged(recv_ref, NB)
    for a in range(NA):
        col[a] = column_form(u_ref[a : a + 1])
    acc[...] = jnp.zeros((NA, TILE, TILE), F32)

    def build(k, a, b):
        value = jnp.exp(xbuf[k] + col[a] + v_ref[pl.ds(b, 1)])
        kbuf[k] = value
        acc[a] += value

    each_tile(list_ref, build)
    for a in range(NA):
        row = row_form(acc[a])
        for d in range(16):
            send_ref[d, a : a + 1] = row


def columns_kernel(list_ref, recv_ref, mass_ref, kbuf, _, send_ref, *rest):
    *kept, col, acc = rest
    alpha = jnp.where(live_rows(list_ref), jnp.exp(mass_ref[...]) / total(recv_ref, 0, NA), 1.0)
    for ref in kept:
        ref[...] = alpha
    for a in range(NA):
        col[a] = column_form(alpha[a : a + 1])
    acc[...] = jnp.zeros((NB, 8, TILE), F32)

    def add(k, a, b):
        acc[b] += fold(kbuf[k] * col[a])

    each_tile(list_ref, add)
    write_copies(send_ref, NB, jnp.sum(acc[...], axis=1))


def rows_kernel(list_ref, recv_ref, mass_ref, kbuf, _, send_ref, beta_ref, acc):
    beta_ref[...] = jnp.exp(mass_ref[...]) / total(recv_ref, 0, NB)
    acc[...] = jnp.zeros((NA, TILE, TILE), F32)

    def add(k, a, b):
        acc[a] += kbuf[k] * beta_ref[pl.ds(b, 1)]

    each_tile(list_ref, add)
    for a in range(NA):
        row = row_form(acc[a])
        for d in range(16):
            send_ref[d, a : a + 1] = row


def masses_kernel(
    list_ref, recv_ref, mass_ref, kbuf, xbuf,
    send_ref, beta_ref, sum_ref, cost_ref,
    acc, acc_cost,
):
    column_sum = total(recv_ref, 0, NB)
    sum_ref[...] = column_sum
    beta_ref[...] = jnp.exp(mass_ref[...]) / column_sum
    acc[...] = jnp.zeros((NA, TILE, TILE), F32)
    acc_cost[...] = jnp.zeros((NA, TILE, TILE), F32)

    def add(k, a, b):
        plan = kbuf[k] * beta_ref[pl.ds(b, 1)]
        acc[a] += plan
        acc_cost[a] += plan * xbuf[k]

    each_tile(list_ref, add)
    for a in range(NA):
        row = row_form(acc[a])
        cost = row_form(acc_cost[a])
        cost_ref[a : a + 1] = cost
        for d in range(16):
            send_ref[d, a : a + 1] = row
            send_ref[d, NA + a : NA + a + 1] = cost


def first_ratio_kernel(
    list_ref, recv_ref, alpha_ref, kbuf, xbuf,
    send_ref, sum_ref, cost_ref,
    col, col2, acc, acc2,
):
    row_sum = total(recv_ref, 0, NA)
    sum_ref[...] = row_sum
    s = jnp.where(live_rows(list_ref), -total(recv_ref, NA, NA) / row_sum, 0.0)
    for a in range(NA):
        col[a] = column_form(alpha_ref[a : a + 1])
        col2[a] = column_form(s[a : a + 1] * damping)
    acc[...] = jnp.zeros((NB, 8, TILE), F32)
    acc2[...] = jnp.zeros((NB, 8, TILE), F32)

    def add(k, a, b):
        plan = kbuf[k] * col[a]
        acc[b] += fold(plan * xbuf[k])
        acc2[b] += fold(plan * (xbuf[k] + col2[a]))

    each_tile(list_ref, add)
    cost_ref[...] = jnp.sum(acc[...], axis=1)
    write_copies(send_ref, NB, jnp.sum(acc2[...], axis=1))


def pull_kernel(
    list_ref, recv_ref, sum_ref, beta_ref, cost_ref, kbuf, _,
    send_ref,
    acc, weight,
):
    t = -total(recv_ref, 0, NB) / sum_ref[...]
    weight[...] = beta_ref[...] * t * damping
    acc[...] = jnp.zeros((NA, TILE, TILE), F32)

    def add(k, a, b):
        acc[a] += kbuf[k] * weight[pl.ds(b, 1)]

    each_tile(list_ref, add)
    for a in range(NA):
        row = cost_ref[a : a + 1] + row_form(acc[a])
        for d in range(16):
            send_ref[d, a : a + 1] = row


def push_kernel(
    list_ref, recv_ref, sum_ref, alpha_ref, cost_ref, kbuf, _,
    send_ref, *rest,
):
    *kept, col, acc = rest
    s = jnp.where(live_rows(list_ref), -total(recv_ref, 0, NA) / sum_ref[...], 0.0)
    for ref in kept:
        ref[...] = s
    weight = alpha_ref[...] * s * damping
    for a in range(NA):
        col[a] = column_form(weight[a : a + 1])
    acc[...] = jnp.zeros((NB, 8, TILE), F32)

    def add(k, a, b):
        acc[b] += fold(kbuf[k] * col[a])

    each_tile(list_ref, add)
    write_copies(send_ref, NB, cost_ref[...] + jnp.sum(acc[...], axis=1))


def gradient_kernel(
    list_ref, recv_ref, sum_ref, beta_ref, alpha_ref, s_ref, u_ref, v_ref,
    cells_ref, t0, t1, t2, t3, xbuf,
    g_ref, source_ref, target_ref,
    tbuf, col, col2, trow, vrow, prod, wbuf, pbuf, sem,
):
    pulls = pulls_of((t0, t1, t2, t3), tbuf, sem)
    for pull in pulls:
        pull.start()
    part = part_index()
    own = pl.ds(lax.axis_index("x") * 4 + lax.axis_index("zh"), 1)
    u = u_ref[...] + jnp.log(alpha_ref[...])
    vrow[...] = v_ref[...] + jnp.log(beta_ref[...])
    source_ref[...] = entropy * (u_ref[own] + jnp.log(alpha_ref[own]))
    own = pl.ds(pl.multiple_of(part * TB_DEV, TB_DEV), TB_DEV)
    target_ref[...] = entropy * vrow[own]
    trow[...] = -total(recv_ref, 0, NB) / sum_ref[...]
    for a in range(NA):
        col[a] = column_form(u[a : a + 1])
        col2[a] = column_form(1.0 + s_ref[a : a + 1])
    prod[...] = jnp.zeros((NA * TILE, D), F32)
    for pull in pulls:
        pull.wait()

    def weigh(step, k, a, b):
        x = xbuf[k]
        weights = jnp.exp(x + col[a] + vrow[pl.ds(b, 1)]) * (x + col2[a] + trow[pl.ds(b, 1)])
        wbuf[step] = weights.astype(jnp.bfloat16)

    def multiply(step, k, a, b):
        slot = jnp.bitwise_xor(lax.shift_right_logical(b, 3), part)
        rows = pl.ds(pl.multiple_of(jnp.bitwise_and(b, TB_DEV - 1) * TILE, TILE), TILE)
        pbuf[step] = jnp.dot(wbuf[step], tbuf[slot, rows, :], preferred_element_type=F32)

    def add(step, k, a, b):
        prod[pl.ds(pl.multiple_of(a * TILE, TILE), TILE)] += pbuf[step]

    each_chunk(list_ref, (weigh, multiply, add))
    g = jnp.zeros((D, D), F32)
    for step in range(3):
        piece = prod[...].astype(jnp.bfloat16)
        if step < 2:
            prod[...] -= piece.astype(F32)
        g += lax.dot_general(cells_ref[...], piece, (((0,), (0,)), ((), ())), preferred_element_type=F32)
    g_ref[...] = g * (-1.0 / math.sqrt(D))


def swap(value, axis):
    return lax.ppermute(value, axis, [(0, 1), (1, 0)])


def row_exchange(value):
    return lax.all_to_all(value, ROW, 0, 0)


def col_exchange(value):
    return lax.all_to_all(value, COL, 0, 0)


def shards(
    source_cells,
    target_cells,
    mapping,
    source_logmass,
    target_logmass,
    group_blocks,
    tile_source,
    tile_target,
):
    codes = jnp.where(tile_source >= 0, tile_source * TB_DEV + tile_target, -1)
    head = jnp.concatenate([codes, group_blocks.reshape(1, 4)], axis=1).astype(F32)
    note = jnp.concatenate(
        [jnp.pad(head, ((0, 7), (0, TILE - TILES - 4))), target_logmass.astype(F32).reshape(TB_DEV, TILE)]
    )
    first = (
        lax.all_to_all(jnp.broadcast_to(source_cells[None], (4, TILE, D)), "zh", 0, 0),
        swap(note, "zl"),
        swap(note, "core"),
        swap(target_cells, "core"),
        source_logmass.astype(F32).reshape(1, TILE),
        target_cells,
    )
    column_cells, note2, note1, t1, own_mass, t0 = lax.optimization_barrier(first)
    t2 = swap(t0, "zl")
    notes = (note, note1, note2, swap(note2, "core"))
    targets = (target_cells, t1, t2, swap(t2, "core"))
    cells = lax.all_to_all(jnp.broadcast_to(column_cells[None], (4, 4, TILE, D)), "x", 0, 0)
    cells = cells.reshape(NA * TILE, D)

    rows_to = (VM, SHAPE((16, NA, TILE), F32))
    cols_to = (VM, SHAPE((16, NB, TILE), F32))
    rows_state = (VM, SHAPE((NA, TILE), F32))
    cols_state = (VM, SHAPE((NB, TILE), F32))
    tiles = (HERE, SHAPE((SLOTS, TILE, TILE), F32))
    row_blocks = pltpu.VMEM((NA, TILE, TILE), F32)
    col_rows = pltpu.VMEM((NB, 8, TILE), F32)
    gathered = pltpu.VMEM((4, TB_DEV * TILE, D), jnp.bfloat16)
    gathered_sems = pltpu.SemaphoreType.DMA((5,))
    gathered_refs = [(VM, cells), (FAR, targets[0]), *[(ANY, value) for value in targets[1:]]]

    (tile_list,) = call(
        plan_kernel,
        "plan",
        [(SM, note) for note in notes],
        [(SM, SHAPE((SLOTS + 8,), jnp.int32))],
        [],
    )
    send, x, k = call(
        scores_kernel,
        "scores",
        [
            (SM, tile_list), *gathered_refs,
            (FAR, mapping), (VM, own_mass),
        ],
        [(VM, SHAPE((16, NA + 8, TILE), F32)), tiles, tiles],
        [
            gathered, pltpu.VMEM((D, D), jnp.bfloat16), pltpu.VMEM((NA * TILE, D), jnp.bfloat16),
            row_blocks, row_blocks, gathered_sems,
        ],
    )
    tile_list, x = (SM, tile_list), (HERE, x)
    recv = row_exchange(send)
    send, u, source_mass = call(
        first_targets_kernel,
        "first_targets",
        [tile_list, (VM, recv), x, (HERE, k)],
        [cols_to, rows_state, rows_state],
        [row_blocks, col_rows, col_rows],
    )
    recv = col_exchange(send)
    send, v, target_mass, k = call(
        kernel_matrix_kernel,
        "kernel_matrix",
        [tile_list, (VM, recv), (VM, u), *[(VM, note) for note in notes], x, (HERE, k)],
        [rows_to, cols_state, cols_state, tiles],
        [row_blocks, row_blocks],
        aliases={8: 3},
    )
    k = (HERE, k)
    for sweep in range(1, SINK):
        recv = row_exchange(send)
        send, *kept = call(
            columns_kernel,
            "columns",
            [tile_list, (VM, recv), (VM, source_mass), k, x],
            [cols_to, *([rows_state] if sweep == SINK - 1 else [])],
            [row_blocks, col_rows],
        )
        recv = col_exchange(send)
        if sweep < SINK - 1:
            (send,) = call(
                rows_kernel,
                "rows",
                [tile_list, (VM, recv), (VM, target_mass), k, x],
                [rows_to],
                [pltpu.VMEM((NB, TILE), F32), row_blocks],
            )
    (alpha,) = kept
    send, beta, column_sum, row_cost = call(
        masses_kernel,
        "masses",
        [tile_list, (VM, recv), (VM, target_mass), k, x],
        [(VM, SHAPE((16, 2 * NA, TILE), F32)), cols_state, cols_state, rows_state],
        [row_blocks, row_blocks],
    )
    recv = row_exchange(send)
    send, row_sum, column_cost = call(
        first_ratio_kernel,
        "first_ratio",
        [tile_list, (VM, recv), (VM, alpha), k, x],
        [cols_to, rows_state, cols_state],
        [row_blocks, row_blocks, col_rows, col_rows],
    )
    recv = col_exchange(send)
    for step in range(1, ADJ):
        (send,) = call(
            pull_kernel,
            "pull",
            [tile_list, (VM, recv), (VM, column_sum), (VM, beta), (VM, row_cost), k, x],
            [rows_to],
            [row_blocks, pltpu.VMEM((NB, TILE), F32)],
        )
        recv = row_exchange(send)
        send, *kept = call(
            push_kernel,
            "push",
            [tile_list, (VM, recv), (VM, row_sum), (VM, alpha), (VM, column_cost), k, x],
            [cols_to, *([rows_state] if step == ADJ - 1 else [])],
            [row_blocks, col_rows],
        )
        recv = col_exchange(send)
    (s,) = kept
    gradient, own_source, own_target = call(
        gradient_kernel,
        "gradient",
        [
            tile_list, (VM, recv), (VM, column_sum), (VM, beta), (VM, alpha), (VM, s), (VM, u), (VM, v),
            *gathered_refs, x,
        ],
        [(VM, SHAPE((D, D), F32)), (VM, SHAPE((1, TILE), F32)), (VM, SHAPE((TB_DEV, TILE), F32))],
        [
            gathered, row_blocks, row_blocks, pltpu.VMEM((NB, TILE), F32), pltpu.VMEM((NB, TILE), F32),
            pltpu.VMEM((NA * TILE, D), F32),
            pltpu.VMEM((CHUNK, TILE, TILE), jnp.bfloat16), pltpu.VMEM((CHUNK, TILE, D), F32), gathered_sems,
        ],
    )
    piece = jnp.sum(col_exchange(gradient.reshape(16, 16, D)), axis=0)
    piece = jnp.sum(row_exchange(jnp.broadcast_to(piece[None], (16, 16, D))), axis=0)
    map_gradient = col_exchange(jnp.broadcast_to(piece[None], (16, 16, D))).reshape(D, D)

    return (own_source.reshape(TILE), own_target.reshape(TB_DEV * TILE), map_gradient)


def solution(mesh):
    grid = Mesh(mesh.devices.reshape(4, 4, 4, 2, 2), AXES)
    tgt = ("x", "zh", "zl", "core")
    both = ("src", *tgt)
    in_specs = (
        P(both, None),
        P(tgt, None),
        P(),
        P(both),
        P(tgt),
        P(),
        P(both, None),
        P(both, None),
    )
    out_specs = (P(both), P(tgt), P())
    return jax.shard_map(shards, mesh=grid, in_specs=in_specs, out_specs=out_specs, check_vma=False)
```

```python
import math

import jax
import jax.numpy as jnp
from jax import lax
from jax.experimental import pallas as pl
from jax.experimental.pallas import tpu as pltpu
from jax.sharding import Mesh, PartitionSpec as P

TILE = 128
TB_DEV = 8
TILES = 64
SINK = 4
ADJ = 4
D = 256

entropy = 0.5
damping = 0.8
lowest = -1e30

AXES = ("src", "x", "zh", "zl", "core")
ROW = ("x", "zh")
COL = ("src", "zl", "core")
NA = 16
NB = 32
SLOTS = 4 * TILES
CHUNK = 8
F32 = jnp.float32


VM = pl.BlockSpec(memory_space=pltpu.VMEM)
SM = pl.BlockSpec(memory_space=pltpu.SMEM)
ANY = pl.BlockSpec(memory_space=pl.ANY)
SHAPE = jax.ShapeDtypeStruct


HERE = "here"
KEPT = "kept"
FAR = "far"


SPACES = {HERE: pltpu.VMEM, KEPT: pltpu.SMEM, FAR: pltpu.HBM}


def call(kernel, name, ins, outs, scratch, flops=2 << 20, moved=1 << 20, vmem=10, aliases={}):
    in_specs, args = [], []
    for spec, value in ins:
        if isinstance(spec, str):
            space = SPACES[spec]
            spec, value = pl.BlockSpec(memory_space=space), pltpu.with_memory_space_constraint(value, space)
        in_specs.append(spec)
        args.append(value)
    outs = [
        (pl.BlockSpec(memory_space=SPACES[spec]), SPACES[spec](shape.shape, shape.dtype)) if isinstance(spec, str) else (spec, shape)
        for spec, shape in outs
    ]
    return pl.pallas_call(
        kernel,
        out_shape=[shape for _, shape in outs],
        in_specs=in_specs,
        out_specs=[spec for spec, _ in outs],
        scratch_shapes=scratch,
        input_output_aliases=aliases,
        name=name,
        cost_estimate=pl.CostEstimate(flops=flops, bytes_accessed=moved, transcendentals=0),
        compiler_params=pltpu.CompilerParams(vmem_limit_bytes=vmem << 20),
    )(*args)


def row_form(block):
    return jnp.sum(block.T, axis=0, keepdims=True)


def column_form(row):
    return jnp.broadcast_to(row, (TILE, TILE)).T


def fold(block):
    return jnp.sum(block.reshape(16, 8, TILE), axis=0)


def fold_max(block):
    return jnp.max(block.reshape(16, 8, TILE), axis=0)


def each_tile(list_ref, body):
    def one(c, carry):
        for step in range(CHUNK):
            k = c * CHUNK + step
            code = list_ref[k]
            body(k, lax.shift_right_logical(code, 5), jnp.bitwise_and(code, NB - 1))
        return carry

    lax.fori_loop(0, lax.shift_right_logical(list_ref[SLOTS] + (CHUNK - 1), 3), one, 0)


def each_chunk(list_ref, bodies):
    def one(c, carry):
        codes = [list_ref[c * CHUNK + step] for step in range(CHUNK)]
        for body in bodies:
            for step, code in enumerate(codes):
                body(step, c * CHUNK + step, lax.shift_right_logical(code, 5), jnp.bitwise_and(code, NB - 1))
        return carry

    lax.fori_loop(0, lax.shift_right_logical(list_ref[SLOTS] + (CHUNK - 1), 3), one, 0)


def part_index():
    return lax.axis_index("zl") * 2 + lax.axis_index("core")


def pulls_of(targets, tbuf, sem):
    return [pltpu.make_async_copy(target, tbuf.at[r], sem.at[r]) for r, target in enumerate(targets)]


def write_copies(out_ref, rows, value, first=0):
    for d in range(16):
        out_ref[d, first : first + rows] = value


def live_rows(list_ref):
    block = 4 * lax.broadcasted_iota(jnp.int32, (NA, TILE), 0) + part_index()
    return block < list_ref[SLOTS + 1]


def total(recv_ref, first, rows):
    so_far = recv_ref[0, first : first + rows]
    for d in range(1, 16):
        so_far = so_far + recv_ref[d, first : first + rows]
    return so_far


def merged(recv_ref, rows):
    largest = recv_ref[0, 0:rows]
    for d in range(1, 16):
        largest = jnp.maximum(largest, recv_ref[d, 0:rows])
    so_far = jnp.zeros((rows, TILE), F32)
    for d in range(16):
        so_far = so_far + jnp.exp(recv_ref[d, 0:rows] - largest)
    return largest + jnp.log(so_far)


def finish_log(largest, so_far):
    good = so_far > 0
    return jnp.where(good, largest + jnp.log(jnp.where(good, so_far, 1.0)), lowest)


def plan_kernel(notes0, notes1, notes2, notes3, list_ref):
    part = part_index()
    count = 0
    for r, notes in enumerate((notes0, notes1, notes2, notes3)):
        base = jnp.bitwise_xor(part, r) * TB_DEV

        def gather(k, n, notes=notes, base=base):
            code = notes[0, k].astype(jnp.int32)
            source = lax.shift_right_arithmetic(code, 3)
            take = jnp.logical_and(code >= 0, jnp.bitwise_and(source, 3) == part)
            target = base + jnp.bitwise_and(code, TB_DEV - 1)
            list_ref[n] = lax.shift_right_arithmetic(source, 2) * NB + target
            return n + take.astype(jnp.int32)

        count = lax.fori_loop(0, TILES, gather, count, unroll=8)

    def clear(k, carry):
        list_ref[k] = 0
        return carry

    lax.fori_loop(count, jnp.minimum(count + CHUNK, SLOTS), clear, 0)
    list_ref[SLOTS] = count
    list_ref[SLOTS + 1] = notes0[0, TILES + lax.axis_index("src")].astype(jnp.int32)


def scores_kernel(
    list_ref, cells_ref, t0, t1, t2, t3, mapping_far, mass_ref,
    send_ref, xbuf, _,
    tbuf, mapping_ref, mapped, top, acc, sem,
):
    pull_mapping = pltpu.make_async_copy(mapping_far, mapping_ref, sem.at[4])
    pull_mapping.start()
    pulls = pulls_of((t0, t1, t2, t3), tbuf, sem)
    for pull in pulls:
        pull.start()
    part = part_index()
    count = list_ref[SLOTS]
    top[...] = jnp.full((NA, TILE, TILE), lowest, F32)
    acc[...] = jnp.zeros((NA, TILE, TILE), F32)
    pull_mapping.wait()

    def embed(step, carry):
        rows = pl.ds(pl.multiple_of(step * 2 * D, 2 * D), 2 * D)
        product = jnp.dot(cells_ref[rows], mapping_ref[...], preferred_element_type=F32)
        mapped[rows] = product.astype(jnp.bfloat16)
        return carry

    lax.fori_loop(0, NA * TILE // (2 * D), embed, 0)
    for pull in pulls:
        pull.wait()
    scale = (1.0 / entropy) / math.sqrt(D)

    def product(step, k, a, b):
        slot = jnp.bitwise_xor(lax.shift_right_logical(b, 3), part)
        rows = pl.ds(pl.multiple_of(jnp.bitwise_and(b, TB_DEV - 1) * TILE, TILE), TILE)
        x = lax.dot_general(
            mapped[pl.ds(pl.multiple_of(a * TILE, TILE), TILE)], tbuf[slot, rows, :], (((1,), (1,)), ((), ())), preferred_element_type=F32
        )
        xbuf[k] = jnp.where(k < count, x * scale, lowest)

    def largest(step, k, a, b):
        top[a] = jnp.maximum(top[a], xbuf[k])

    each_chunk(list_ref, (product, largest))

    def spread(a, carry):
        top[a] = jnp.broadcast_to(jnp.max(top[a], axis=1, keepdims=True), (TILE, TILE))
        return carry

    lax.fori_loop(0, NA, spread, 0)

    def add(k, a, b):
        acc[a] += jnp.exp(xbuf[k] - top[a])

    each_tile(list_ref, add)
    for a in range(NA):
        row = finish_log(top[a].T[0:1], row_form(acc[a]))
        for d in range(16):
            send_ref[d, a : a + 1] = row
    write_copies(send_ref, 8, jnp.broadcast_to(mass_ref[...], (8, TILE)), NA)


def first_targets_kernel(
    list_ref, recv_ref, xbuf, _,
    send_ref, u_ref, mass_out,
    col, top, acc,
):
    for a in range(NA):
        mass_out[a : a + 1] = recv_ref[a, NA : NA + 1]
    u = jnp.where(live_rows(list_ref), mass_out[...] - merged(recv_ref, NA), 0.0)
    u_ref[...] = u
    for a in range(NA):
        col[a] = column_form(u[a : a + 1])
    top[...] = jnp.full((NB, 8, TILE), lowest, F32)
    acc[...] = jnp.zeros((NB, 8, TILE), F32)

    def largest(k, a, b):
        top[b] = jnp.maximum(top[b], fold_max(xbuf[k] + col[a]))

    each_tile(list_ref, largest)
    for b in range(NB):
        top[b] = jnp.broadcast_to(jnp.max(top[b], axis=0, keepdims=True), (8, TILE))

    def add(k, a, b):
        acc[b] += fold(jnp.exp(xbuf[k] + col[a] - top[b][0:1]))

    each_tile(list_ref, add)
    for b in range(NB):
        row = finish_log(top[b][0:1], jnp.sum(acc[b], axis=0, keepdims=True))
        for d in range(16):
            send_ref[d, b : b + 1] = row


def kernel_matrix_kernel(
    list_ref, recv_ref, u_ref, notes0, notes1, notes2, notes3, xbuf, _,
    send_ref, v_ref, mass_out, kbuf,
    col, acc,
):
    for r, notes in enumerate((notes0, notes1, notes2, notes3)):
        first = pl.multiple_of(jnp.bitwise_xor(part_index(), r) * TB_DEV, TB_DEV)
        mass_out[pl.ds(first, TB_DEV)] = notes[TB_DEV : 2 * TB_DEV]
    v_ref[...] = mass_out[...] - merged(recv_ref, NB)
    for a in range(NA):
        col[a] = column_form(u_ref[a : a + 1])
    acc[...] = jnp.zeros((NA, TILE, TILE), F32)

    def build(k, a, b):
        value = jnp.exp(xbuf[k] + col[a] + v_ref[pl.ds(b, 1)])
        kbuf[k] = value
        acc[a] += value

    each_tile(list_ref, build)
    for a in range(NA):
        row = row_form(acc[a])
        for d in range(16):
            send_ref[d, a : a + 1] = row


def columns_kernel(list_ref, recv_ref, mass_ref, kbuf, _, send_ref, *rest):
    *kept, col, acc = rest
    alpha = jnp.where(live_rows(list_ref), jnp.exp(mass_ref[...]) / total(recv_ref, 0, NA), 1.0)
    for ref in kept:
        ref[...] = alpha
    for a in range(NA):
        col[a] = column_form(alpha[a : a + 1])
    acc[...] = jnp.zeros((NB, 8, TILE), F32)

    def add(k, a, b):
        acc[b] += fold(kbuf[k] * col[a])

    each_tile(list_ref, add)
    write_copies(send_ref, NB, jnp.sum(acc[...], axis=1))


def rows_kernel(list_ref, recv_ref, mass_ref, kbuf, _, send_ref, beta_ref, acc):
    beta_ref[...] = jnp.exp(mass_ref[...]) / total(recv_ref, 0, NB)
    acc[...] = jnp.zeros((NA, TILE, TILE), F32)

    def add(k, a, b):
        acc[a] += kbuf[k] * beta_ref[pl.ds(b, 1)]

    each_tile(list_ref, add)
    for a in range(NA):
        row = row_form(acc[a])
        for d in range(16):
            send_ref[d, a : a + 1] = row


def masses_kernel(
    list_ref, recv_ref, mass_ref, kbuf, xbuf,
    send_ref, beta_ref, sum_ref, cost_ref,
    acc, acc_cost,
):
    column_sum = total(recv_ref, 0, NB)
    sum_ref[...] = column_sum
    beta_ref[...] = jnp.exp(mass_ref[...]) / column_sum
    acc[...] = jnp.zeros((NA, TILE, TILE), F32)
    acc_cost[...] = jnp.zeros((NA, TILE, TILE), F32)

    def add(k, a, b):
        plan = kbuf[k] * beta_ref[pl.ds(b, 1)]
        acc[a] += plan
        acc_cost[a] += plan * xbuf[k]

    each_tile(list_ref, add)
    for a in range(NA):
        row = row_form(acc[a])
        cost = row_form(acc_cost[a])
        cost_ref[a : a + 1] = cost
        for d in range(16):
            send_ref[d, a : a + 1] = row
            send_ref[d, NA + a : NA + a + 1] = cost


def first_ratio_kernel(
    list_ref, recv_ref, alpha_ref, kbuf, xbuf,
    send_ref, sum_ref, cost_ref,
    col, col2, acc, acc2,
):
    row_sum = total(recv_ref, 0, NA)
    sum_ref[...] = row_sum
    s = jnp.where(live_rows(list_ref), -total(recv_ref, NA, NA) / row_sum, 0.0)
    for a in range(NA):
        col[a] = column_form(alpha_ref[a : a + 1])
        col2[a] = column_form(s[a : a + 1] * damping)
    acc[...] = jnp.zeros((NB, 8, TILE), F32)
    acc2[...] = jnp.zeros((NB, 8, TILE), F32)

    def add(k, a, b):
        plan = kbuf[k] * col[a]
        acc[b] += fold(plan * xbuf[k])
        acc2[b] += fold(plan * (xbuf[k] + col2[a]))

    each_tile(list_ref, add)
    cost_ref[...] = jnp.sum(acc[...], axis=1)
    write_copies(send_ref, NB, jnp.sum(acc2[...], axis=1))


def pull_kernel(
    list_ref, recv_ref, sum_ref, beta_ref, cost_ref, kbuf, _,
    send_ref,
    acc, weight,
):
    t = -total(recv_ref, 0, NB) / sum_ref[...]
    weight[...] = beta_ref[...] * t * damping
    acc[...] = jnp.zeros((NA, TILE, TILE), F32)

    def add(k, a, b):
        acc[a] += kbuf[k] * weight[pl.ds(b, 1)]

    each_tile(list_ref, add)
    for a in range(NA):
        row = cost_ref[a : a + 1] + row_form(acc[a])
        for d in range(16):
            send_ref[d, a : a + 1] = row


def push_kernel(
    list_ref, recv_ref, sum_ref, alpha_ref, cost_ref, kbuf, _,
    send_ref, *rest,
):
    *kept, col, acc = rest
    s = jnp.where(live_rows(list_ref), -total(recv_ref, 0, NA) / sum_ref[...], 0.0)
    for ref in kept:
        ref[...] = s
    weight = alpha_ref[...] * s * damping
    for a in range(NA):
        col[a] = column_form(weight[a : a + 1])
    acc[...] = jnp.zeros((NB, 8, TILE), F32)

    def add(k, a, b):
        acc[b] += fold(kbuf[k] * col[a])

    each_tile(list_ref, add)
    write_copies(send_ref, NB, cost_ref[...] + jnp.sum(acc[...], axis=1))


def gradient_kernel(
    list_ref, recv_ref, sum_ref, beta_ref, alpha_ref, s_ref, u_ref, v_ref,
    cells_ref, t0, t1, t2, t3, xbuf,
    g_ref, source_ref, target_ref,
    tbuf, col, col2, trow, vrow, prod, wbuf, pbuf, sem,
):
    pulls = pulls_of((t0, t1, t2, t3), tbuf, sem)
    for pull in pulls:
        pull.start()
    part = part_index()
    own = pl.ds(lax.axis_index("x") * 4 + lax.axis_index("zh"), 1)
    u = u_ref[...] + jnp.log(alpha_ref[...])
    vrow[...] = v_ref[...] + jnp.log(beta_ref[...])
    source_ref[...] = entropy * (u_ref[own] + jnp.log(alpha_ref[own]))
    own = pl.ds(pl.multiple_of(part * TB_DEV, TB_DEV), TB_DEV)
    target_ref[...] = entropy * vrow[own]
    trow[...] = -total(recv_ref, 0, NB) / sum_ref[...]
    for a in range(NA):
        col[a] = column_form(u[a : a + 1])
        col2[a] = column_form(1.0 + s_ref[a : a + 1])
    prod[...] = jnp.zeros((NA * TILE, D), F32)
    for pull in pulls:
        pull.wait()

    def weigh(step, k, a, b):
        x = xbuf[k]
        weights = jnp.exp(x + col[a] + vrow[pl.ds(b, 1)]) * (x + col2[a] + trow[pl.ds(b, 1)])
        wbuf[step] = weights.astype(jnp.bfloat16)

    def multiply(step, k, a, b):
        slot = jnp.bitwise_xor(lax.shift_right_logical(b, 3), part)
        rows = pl.ds(pl.multiple_of(jnp.bitwise_and(b, TB_DEV - 1) * TILE, TILE), TILE)
        pbuf[step] = jnp.dot(wbuf[step], tbuf[slot, rows, :], preferred_element_type=F32)

    def add(step, k, a, b):
        prod[pl.ds(pl.multiple_of(a * TILE, TILE), TILE)] += pbuf[step]

    each_chunk(list_ref, (weigh, multiply, add))
    g = jnp.zeros((D, D), F32)
    for step in range(3):
        piece = prod[...].astype(jnp.bfloat16)
        if step < 2:
            prod[...] -= piece.astype(F32)
        g += lax.dot_general(cells_ref[...], piece, (((0,), (0,)), ((), ())), preferred_element_type=F32)
    g_ref[...] = g * (-1.0 / math.sqrt(D))


def swap(value, axis):
    return lax.ppermute(value, axis, [(0, 1), (1, 0)])


def row_exchange(value):
    return lax.all_to_all(value, ROW, 0, 0)


def col_exchange(value):
    return lax.all_to_all(value, COL, 0, 0)


def shards(
    source_cells,
    target_cells,
    mapping,
    source_logmass,
    target_logmass,
    group_blocks,
    tile_source,
    tile_target,
):
    codes = jnp.where(tile_source >= 0, tile_source * TB_DEV + tile_target, -1)
    head = jnp.concatenate([codes, group_blocks.reshape(1, 4)], axis=1).astype(F32)
    note = jnp.concatenate(
        [jnp.pad(head, ((0, 7), (0, TILE - TILES - 4))), target_logmass.astype(F32).reshape(TB_DEV, TILE)]
    )
    note2 = swap(note, "zl")
    first = (
        lax.all_to_all(jnp.broadcast_to(source_cells[None], (4, TILE, D)), "zh", 0, 0),
        note2,
        swap(note2, "core"),
        swap(note, "core"),
        swap(target_cells, "core"),
        source_logmass.astype(F32).reshape(1, TILE),
        target_cells,
    )
    column_cells, note2, note3, note1, t1, own_mass, t0 = lax.optimization_barrier(first)
    t2 = swap(t0, "zl")
    notes = (note, note1, note2, note3)
    targets = (target_cells, t1, t2, swap(t2, "core"))
    cells = lax.all_to_all(jnp.broadcast_to(column_cells[None], (4, 4, TILE, D)), "x", 0, 0)
    cells = cells.reshape(NA * TILE, D)

    rows_to = (VM, SHAPE((16, NA, TILE), F32))
    cols_to = (VM, SHAPE((16, NB, TILE), F32))
    rows_state = (VM, SHAPE((NA, TILE), F32))
    cols_state = (VM, SHAPE((NB, TILE), F32))
    tiles = (HERE, SHAPE((SLOTS, TILE, TILE), F32))
    row_blocks = pltpu.VMEM((NA, TILE, TILE), F32)
    col_rows = pltpu.VMEM((NB, 8, TILE), F32)
    gathered = pltpu.VMEM((4, TB_DEV * TILE, D), jnp.bfloat16)
    gathered_sems = pltpu.SemaphoreType.DMA((5,))
    gathered_refs = [(VM, cells), (FAR, targets[0]), *[(ANY, value) for value in targets[1:]]]

    (tile_list,) = call(
        plan_kernel,
        "plan",
        [(SM, note) for note in notes],
        [(KEPT, SHAPE((SLOTS + 8,), jnp.int32))],
        [],
        moved=10 << 20,
    )
    send, x, k = call(
        scores_kernel,
        "scores",
        [
            (KEPT, tile_list), *gathered_refs,
            (FAR, mapping), (VM, own_mass),
        ],
        [(VM, SHAPE((16, NA + 8, TILE), F32)), tiles, tiles],
        [
            gathered, pltpu.VMEM((D, D), jnp.bfloat16), pltpu.VMEM((NA * TILE, D), jnp.bfloat16),
            row_blocks, row_blocks, gathered_sems,
        ],
    )
    tile_list, x = (KEPT, tile_list), (HERE, x)
    recv = row_exchange(send)
    send, u, source_mass = call(
        first_targets_kernel,
        "first_targets",
        [tile_list, (VM, recv), x, (HERE, k)],
        [cols_to, rows_state, rows_state],
        [row_blocks, col_rows, col_rows],
    )
    recv = col_exchange(send)
    send, v, target_mass, k = call(
        kernel_matrix_kernel,
        "kernel_matrix",
        [tile_list, (VM, recv), (VM, u), *[(VM, note) for note in notes], x, (HERE, k)],
        [rows_to, cols_state, cols_state, tiles],
        [row_blocks, row_blocks],
        aliases={8: 3},
    )
    k = (HERE, k)
    for sweep in range(1, SINK):
        recv = row_exchange(send)
        send, *kept = call(
            columns_kernel,
            "columns",
            [tile_list, (VM, recv), (VM, source_mass), k, x],
            [cols_to, *([rows_state] if sweep == SINK - 1 else [])],
            [row_blocks, col_rows],
        )
        recv = col_exchange(send)
        if sweep < SINK - 1:
            (send,) = call(
                rows_kernel,
                "rows",
                [tile_list, (VM, recv), (VM, target_mass), k, x],
                [rows_to],
                [pltpu.VMEM((NB, TILE), F32), row_blocks],
            )
    (alpha,) = kept
    send, beta, column_sum, row_cost = call(
        masses_kernel,
        "masses",
        [tile_list, (VM, recv), (VM, target_mass), k, x],
        [(VM, SHAPE((16, 2 * NA, TILE), F32)), cols_state, cols_state, rows_state],
        [row_blocks, row_blocks],
    )
    recv = row_exchange(send)
    send, row_sum, column_cost = call(
        first_ratio_kernel,
        "first_ratio",
        [tile_list, (VM, recv), (VM, alpha), k, x],
        [cols_to, rows_state, cols_state],
        [row_blocks, row_blocks, col_rows, col_rows],
    )
    recv = col_exchange(send)
    for step in range(1, ADJ):
        (send,) = call(
            pull_kernel,
            "pull",
            [tile_list, (VM, recv), (VM, column_sum), (VM, beta), (VM, row_cost), k, x],
            [rows_to],
            [row_blocks, pltpu.VMEM((NB, TILE), F32)],
        )
        recv = row_exchange(send)
        send, *kept = call(
            push_kernel,
            "push",
            [tile_list, (VM, recv), (VM, row_sum), (VM, alpha), (VM, column_cost), k, x],
            [cols_to, *([rows_state] if step == ADJ - 1 else [])],
            [row_blocks, col_rows],
        )
        recv = col_exchange(send)
    (s,) = kept
    gradient, own_source, own_target = call(
        gradient_kernel,
        "gradient",
        [
            tile_list, (VM, recv), (VM, column_sum), (VM, beta), (VM, alpha), (VM, s), (VM, u), (VM, v),
            *gathered_refs, x,
        ],
        [(VM, SHAPE((D, D), F32)), (VM, SHAPE((1, TILE), F32)), (VM, SHAPE((TB_DEV, TILE), F32))],
        [
            gathered, row_blocks, row_blocks, pltpu.VMEM((NB, TILE), F32), pltpu.VMEM((NB, TILE), F32),
            pltpu.VMEM((NA * TILE, D), F32),
            pltpu.VMEM((CHUNK, TILE, TILE), jnp.bfloat16), pltpu.VMEM((CHUNK, TILE, D), F32), gathered_sems,
        ],
    )
    piece = jnp.sum(col_exchange(gradient.reshape(16, 16, D)), axis=0)
    piece = jnp.sum(row_exchange(jnp.broadcast_to(piece[None], (16, 16, D))), axis=0)
    map_gradient = col_exchange(jnp.broadcast_to(piece[None], (16, 16, D))).reshape(D, D)

    return (own_source.reshape(TILE), own_target.reshape(TB_DEV * TILE), map_gradient)


def solution(mesh):
    grid = Mesh(mesh.devices.reshape(4, 4, 4, 2, 2), AXES)
    tgt = ("x", "zh", "zl", "core")
    both = ("src", *tgt)
    in_specs = (
        P(both, None),
        P(tgt, None),
        P(),
        P(both),
        P(tgt),
        P(),
        P(both, None),
        P(both, None),
    )
    out_specs = (P(both), P(tgt), P())
    return jax.shard_map(shards, mesh=grid, in_specs=in_specs, out_specs=out_specs, check_vma=False)
```

```python
import math

import jax
import jax.numpy as jnp
from jax import lax
from jax.experimental import pallas as pl
from jax.experimental.pallas import tpu as pltpu
from jax.sharding import Mesh, PartitionSpec as P

TILE = 128
TB_DEV = 8
TILES = 64
SINK = 4
ADJ = 4
D = 256

entropy = 0.5
damping = 0.8
lowest = -1e30

AXES = ("src", "x", "zh", "zl", "core")
ROW = ("x", "zh")
COL = ("src", "zl", "core")
NA = 16
NB = 32
SLOTS = 4 * TILES
CHUNK = 8
F32 = jnp.float32


VM = pl.BlockSpec(memory_space=pltpu.VMEM)
SM = pl.BlockSpec(memory_space=pltpu.SMEM)
ANY = pl.BlockSpec(memory_space=pl.ANY)
SHAPE = jax.ShapeDtypeStruct


HERE = "here"
KEPT = "kept"
FAR = "far"


SPACES = {HERE: pltpu.VMEM, KEPT: pltpu.SMEM, FAR: pltpu.HBM}


def call(kernel, name, ins, outs, scratch, flops=2 << 20, moved=1 << 20, vmem=10, aliases={}):
    in_specs, args = [], []
    for spec, value in ins:
        if isinstance(spec, str):
            space = SPACES[spec]
            spec, value = pl.BlockSpec(memory_space=space), pltpu.with_memory_space_constraint(value, space)
        in_specs.append(spec)
        args.append(value)
    outs = [
        (pl.BlockSpec(memory_space=SPACES[spec]), SPACES[spec](shape.shape, shape.dtype)) if isinstance(spec, str) else (spec, shape)
        for spec, shape in outs
    ]
    return pl.pallas_call(
        kernel,
        out_shape=[shape for _, shape in outs],
        in_specs=in_specs,
        out_specs=[spec for spec, _ in outs],
        scratch_shapes=scratch,
        input_output_aliases=aliases,
        name=name,
        cost_estimate=pl.CostEstimate(flops=flops, bytes_accessed=moved, transcendentals=0),
        compiler_params=pltpu.CompilerParams(vmem_limit_bytes=vmem << 20),
    )(*args)


def row_form(block):
    return jnp.sum(block.T, axis=0, keepdims=True)


def column_form(row):
    return jnp.broadcast_to(row, (TILE, TILE)).T


def fold(block):
    return jnp.sum(block.reshape(16, 8, TILE), axis=0)


def fold_max(block):
    return jnp.max(block.reshape(16, 8, TILE), axis=0)


def each_tile(list_ref, body):
    def one(c, carry):
        for step in range(CHUNK):
            k = c * CHUNK + step
            code = list_ref[k]
            body(k, lax.shift_right_logical(code, 5), jnp.bitwise_and(code, NB - 1))
        return carry

    lax.fori_loop(0, lax.shift_right_logical(list_ref[SLOTS] + (CHUNK - 1), 3), one, 0)


def each_chunk(list_ref, bodies):
    def one(c, carry):
        codes = [list_ref[c * CHUNK + step] for step in range(CHUNK)]
        for body in bodies:
            for step, code in enumerate(codes):
                body(step, c * CHUNK + step, lax.shift_right_logical(code, 5), jnp.bitwise_and(code, NB - 1))
        return carry

    lax.fori_loop(0, lax.shift_right_logical(list_ref[SLOTS] + (CHUNK - 1), 3), one, 0)


def part_index():
    return lax.axis_index("zl") * 2 + lax.axis_index("core")


def pulls_of(targets, tbuf, sem):
    return [pltpu.make_async_copy(target, tbuf.at[r], sem.at[r]) for r, target in enumerate(targets)]


def write_copies(out_ref, rows, value, first=0):
    for d in range(16):
        out_ref[d, first : first + rows] = value


def live_rows(list_ref):
    block = 4 * lax.broadcasted_iota(jnp.int32, (NA, TILE), 0) + part_index()
    return block < list_ref[SLOTS + 1]


def total(recv_ref, first, rows):
    so_far = recv_ref[0, first : first + rows]
    for d in range(1, 16):
        so_far = so_far + recv_ref[d, first : first + rows]
    return so_far


def merged(recv_ref, rows):
    largest = recv_ref[0, 0:rows]
    for d in range(1, 16):
        largest = jnp.maximum(largest, recv_ref[d, 0:rows])
    so_far = jnp.zeros((rows, TILE), F32)
    for d in range(16):
        so_far = so_far + jnp.exp(recv_ref[d, 0:rows] - largest)
    return largest + jnp.log(so_far)


def finish_log(largest, so_far):
    good = so_far > 0
    return jnp.where(good, largest + jnp.log(jnp.where(good, so_far, 1.0)), lowest)


def plan_kernel(notes0, notes1, notes2, notes3, list_ref):
    part = part_index()
    count = 0
    for r, notes in enumerate((notes0, notes1, notes2, notes3)):
        base = jnp.bitwise_xor(part, r) * TB_DEV

        def gather(k, n, notes=notes, base=base):
            code = notes[0, k].astype(jnp.int32)
            source = lax.shift_right_arithmetic(code, 3)
            take = jnp.logical_and(code >= 0, jnp.bitwise_and(source, 3) == part)
            target = base + jnp.bitwise_and(code, TB_DEV - 1)
            list_ref[n] = lax.shift_right_arithmetic(source, 2) * NB + target
            return n + take.astype(jnp.int32)

        count = lax.fori_loop(0, TILES, gather, count, unroll=8)

    def clear(k, carry):
        list_ref[k] = 0
        return carry

    lax.fori_loop(count, jnp.minimum(count + CHUNK, SLOTS), clear, 0)
    list_ref[SLOTS] = count
    list_ref[SLOTS + 1] = notes0[0, TILES + lax.axis_index("src")].astype(jnp.int32)


def scores_kernel(
    list_ref, cells_ref, t0, t1, t2, t3, mapping_far, mass_ref,
    send_ref, xbuf, _,
    tbuf, mapping_ref, mapped, top, acc, sem,
):
    pull_mapping = pltpu.make_async_copy(mapping_far, mapping_ref, sem.at[4])
    pull_mapping.start()
    pulls = pulls_of((t0, t1, t2, t3), tbuf, sem)
    for pull in pulls:
        pull.start()
    part = part_index()
    count = list_ref[SLOTS]
    top[...] = jnp.full((NA, TILE, TILE), lowest, F32)
    acc[...] = jnp.zeros((NA, TILE, TILE), F32)
    pull_mapping.wait()

    def embed(step, carry):
        rows = pl.ds(pl.multiple_of(step * 2 * D, 2 * D), 2 * D)
        product = jnp.dot(cells_ref[rows], mapping_ref[...], preferred_element_type=F32)
        mapped[rows] = product.astype(jnp.bfloat16)
        return carry

    lax.fori_loop(0, NA * TILE // (2 * D), embed, 0)
    for pull in pulls:
        pull.wait()
    scale = (1.0 / entropy) / math.sqrt(D)

    def product(step, k, a, b):
        slot = jnp.bitwise_xor(lax.shift_right_logical(b, 3), part)
        rows = pl.ds(pl.multiple_of(jnp.bitwise_and(b, TB_DEV - 1) * TILE, TILE), TILE)
        x = lax.dot_general(
            mapped[pl.ds(pl.multiple_of(a * TILE, TILE), TILE)], tbuf[slot, rows, :], (((1,), (1,)), ((), ())), preferred_element_type=F32
        )
        xbuf[k] = jnp.where(k < count, x * scale, lowest)

    def largest(step, k, a, b):
        top[a] = jnp.maximum(top[a], xbuf[k])

    each_chunk(list_ref, (product, largest))

    def spread(a, carry):
        top[a] = jnp.broadcast_to(jnp.max(top[a], axis=1, keepdims=True), (TILE, TILE))
        return carry

    lax.fori_loop(0, NA, spread, 0)

    def add(k, a, b):
        acc[a] += jnp.exp(xbuf[k] - top[a])

    each_tile(list_ref, add)
    for a in range(NA):
        row = finish_log(top[a].T[0:1], row_form(acc[a]))
        for d in range(16):
            send_ref[d, a : a + 1] = row
    write_copies(send_ref, 8, jnp.broadcast_to(mass_ref[...], (8, TILE)), NA)


def first_targets_kernel(
    list_ref, recv_ref, xbuf, _,
    send_ref, u_ref, mass_out,
    col, top, acc,
):
    for a in range(NA):
        mass_out[a : a + 1] = recv_ref[a, NA : NA + 1]
    u = jnp.where(live_rows(list_ref), mass_out[...] - merged(recv_ref, NA), 0.0)
    u_ref[...] = u
    for a in range(NA):
        col[a] = column_form(u[a : a + 1])
    top[...] = jnp.full((NB, 8, TILE), lowest, F32)
    acc[...] = jnp.zeros((NB, 8, TILE), F32)

    def largest(k, a, b):
        top[b] = jnp.maximum(top[b], fold_max(xbuf[k] + col[a]))

    each_tile(list_ref, largest)
    for b in range(NB):
        top[b] = jnp.broadcast_to(jnp.max(top[b], axis=0, keepdims=True), (8, TILE))

    def add(k, a, b):
        acc[b] += fold(jnp.exp(xbuf[k] + col[a] - top[b][0:1]))

    each_tile(list_ref, add)
    for b in range(NB):
        row = finish_log(top[b][0:1], jnp.sum(acc[b], axis=0, keepdims=True))
        for d in range(16):
            send_ref[d, b : b + 1] = row


def kernel_matrix_kernel(
    list_ref, recv_ref, u_ref, notes0, notes1, notes2, notes3, xbuf, _,
    send_ref, v_ref, mass_out, kbuf,
    col, acc,
):
    for r, notes in enumerate((notes0, notes1, notes2, notes3)):
        first = pl.multiple_of(jnp.bitwise_xor(part_index(), r) * TB_DEV, TB_DEV)
        mass_out[pl.ds(first, TB_DEV)] = notes[TB_DEV : 2 * TB_DEV]
    v_ref[...] = mass_out[...] - merged(recv_ref, NB)
    for a in range(NA):
        col[a] = column_form(u_ref[a : a + 1])
    acc[...] = jnp.zeros((NA, TILE, TILE), F32)

    def build(k, a, b):
        value = jnp.exp(xbuf[k] + col[a] + v_ref[pl.ds(b, 1)])
        kbuf[k] = value
        acc[a] += value

    each_tile(list_ref, build)
    for a in range(NA):
        row = row_form(acc[a])
        for d in range(16):
            send_ref[d, a : a + 1] = row


def columns_kernel(list_ref, recv_ref, mass_ref, kbuf, _, send_ref, *rest):
    *kept, col, acc = rest
    alpha = jnp.where(live_rows(list_ref), jnp.exp(mass_ref[...]) / total(recv_ref, 0, NA), 1.0)
    for ref in kept:
        ref[...] = alpha
    for a in range(NA):
        col[a] = column_form(alpha[a : a + 1])
    acc[...] = jnp.zeros((NB, 8, TILE), F32)

    def add(k, a, b):
        acc[b] += fold(kbuf[k] * col[a])

    each_tile(list_ref, add)
    write_copies(send_ref, NB, jnp.sum(acc[...], axis=1))


def rows_kernel(list_ref, recv_ref, mass_ref, kbuf, _, send_ref, beta_ref, acc):
    beta_ref[...] = jnp.exp(mass_ref[...]) / total(recv_ref, 0, NB)
    acc[...] = jnp.zeros((NA, TILE, TILE), F32)

    def add(k, a, b):
        acc[a] += kbuf[k] * beta_ref[pl.ds(b, 1)]

    each_tile(list_ref, add)
    for a in range(NA):
        row = row_form(acc[a])
        for d in range(16):
            send_ref[d, a : a + 1] = row


def masses_kernel(
    list_ref, recv_ref, mass_ref, kbuf, xbuf,
    send_ref, beta_ref, sum_ref, cost_ref,
    acc, acc_cost,
):
    column_sum = total(recv_ref, 0, NB)
    sum_ref[...] = column_sum
    beta_ref[...] = jnp.exp(mass_ref[...]) / column_sum
    acc[...] = jnp.zeros((NA, TILE, TILE), F32)
    acc_cost[...] = jnp.zeros((NA, TILE, TILE), F32)

    def add(k, a, b):
        plan = kbuf[k] * beta_ref[pl.ds(b, 1)]
        acc[a] += plan
        acc_cost[a] += plan * xbuf[k]

    each_tile(list_ref, add)
    for a in range(NA):
        row = row_form(acc[a])
        cost = row_form(acc_cost[a])
        cost_ref[a : a + 1] = cost
        for d in range(16):
            send_ref[d, a : a + 1] = row
            send_ref[d, NA + a : NA + a + 1] = cost


def first_ratio_kernel(
    list_ref, recv_ref, alpha_ref, kbuf, xbuf,
    send_ref, sum_ref, cost_ref,
    col, col2, acc, acc2,
):
    row_sum = total(recv_ref, 0, NA)
    sum_ref[...] = row_sum
    s = jnp.where(live_rows(list_ref), -total(recv_ref, NA, NA) / row_sum, 0.0)
    for a in range(NA):
        col[a] = column_form(alpha_ref[a : a + 1])
        col2[a] = column_form(s[a : a + 1] * damping)
    acc[...] = jnp.zeros((NB, 8, TILE), F32)
    acc2[...] = jnp.zeros((NB, 8, TILE), F32)

    def add(k, a, b):
        plan = kbuf[k] * col[a]
        acc[b] += fold(plan * xbuf[k])
        acc2[b] += fold(plan * (xbuf[k] + col2[a]))

    each_tile(list_ref, add)
    cost_ref[...] = jnp.sum(acc[...], axis=1)
    write_copies(send_ref, NB, jnp.sum(acc2[...], axis=1))


def pull_kernel(
    list_ref, recv_ref, sum_ref, beta_ref, cost_ref, kbuf, _,
    send_ref,
    acc, weight,
):
    t = -total(recv_ref, 0, NB) / sum_ref[...]
    weight[...] = beta_ref[...] * t * damping
    acc[...] = jnp.zeros((NA, TILE, TILE), F32)

    def add(k, a, b):
        acc[a] += kbuf[k] * weight[pl.ds(b, 1)]

    each_tile(list_ref, add)
    for a in range(NA):
        row = cost_ref[a : a + 1] + row_form(acc[a])
        for d in range(16):
            send_ref[d, a : a + 1] = row


def push_kernel(
    list_ref, recv_ref, sum_ref, alpha_ref, cost_ref, kbuf, _,
    send_ref, *rest,
):
    *kept, col, acc = rest
    s = jnp.where(live_rows(list_ref), -total(recv_ref, 0, NA) / sum_ref[...], 0.0)
    for ref in kept:
        ref[...] = s
    weight = alpha_ref[...] * s * damping
    for a in range(NA):
        col[a] = column_form(weight[a : a + 1])
    acc[...] = jnp.zeros((NB, 8, TILE), F32)

    def add(k, a, b):
        acc[b] += fold(kbuf[k] * col[a])

    each_tile(list_ref, add)
    write_copies(send_ref, NB, cost_ref[...] + jnp.sum(acc[...], axis=1))


def gradient_kernel(
    list_ref, recv_ref, sum_ref, beta_ref, alpha_ref, s_ref, u_ref, v_ref,
    cells_ref, t0, t1, t2, t3, xbuf,
    g_ref, source_ref, target_ref,
    tbuf, col, col2, trow, vrow, prod, wbuf, pbuf, sem,
):
    pulls = pulls_of((t0, t1, t2, t3), tbuf, sem)
    for pull in pulls:
        pull.start()
    part = part_index()
    own = pl.ds(lax.axis_index("x") * 4 + lax.axis_index("zh"), 1)
    u = u_ref[...] + jnp.log(alpha_ref[...])
    vrow[...] = v_ref[...] + jnp.log(beta_ref[...])
    source_ref[...] = entropy * (u_ref[own] + jnp.log(alpha_ref[own]))
    own = pl.ds(pl.multiple_of(part * TB_DEV, TB_DEV), TB_DEV)
    target_ref[...] = entropy * vrow[own]
    trow[...] = -total(recv_ref, 0, NB) / sum_ref[...]
    for a in range(NA):
        col[a] = column_form(u[a : a + 1])
        col2[a] = column_form(1.0 + s_ref[a : a + 1])
    prod[...] = jnp.zeros((NA * TILE, D), F32)
    for pull in pulls:
        pull.wait()

    def weigh(step, k, a, b):
        x = xbuf[k]
        weights = jnp.exp(x + col[a] + vrow[pl.ds(b, 1)]) * (x + col2[a] + trow[pl.ds(b, 1)])
        wbuf[step] = weights.astype(jnp.bfloat16)

    def multiply(step, k, a, b):
        slot = jnp.bitwise_xor(lax.shift_right_logical(b, 3), part)
        rows = pl.ds(pl.multiple_of(jnp.bitwise_and(b, TB_DEV - 1) * TILE, TILE), TILE)
        pbuf[step] = jnp.dot(wbuf[step], tbuf[slot, rows, :], preferred_element_type=F32)

    def add(step, k, a, b):
        prod[pl.ds(pl.multiple_of(a * TILE, TILE), TILE)] += pbuf[step]

    each_chunk(list_ref, (weigh, multiply, add))
    g = jnp.zeros((D, D), F32)
    for step in range(2):
        piece = prod[...].astype(jnp.bfloat16)
        if step < 1:
            prod[...] -= piece.astype(F32)
        g += lax.dot_general(cells_ref[...], piece, (((0,), (0,)), ((), ())), preferred_element_type=F32)
    g_ref[...] = g * (-1.0 / math.sqrt(D))


def swap(value, axis):
    return lax.ppermute(value, axis, [(0, 1), (1, 0)])


def row_exchange(value):
    return lax.all_to_all(value, ROW, 0, 0)


def col_exchange(value):
    return lax.all_to_all(value, COL, 0, 0)


def shards(
    source_cells,
    target_cells,
    mapping,
    source_logmass,
    target_logmass,
    group_blocks,
    tile_source,
    tile_target,
):
    codes = jnp.where(tile_source >= 0, tile_source * TB_DEV + tile_target, -1)
    head = jnp.concatenate([codes, group_blocks.reshape(1, 4)], axis=1).astype(F32)
    note = jnp.concatenate(
        [jnp.pad(head, ((0, 7), (0, TILE - TILES - 4))), target_logmass.astype(F32).reshape(TB_DEV, TILE)]
    )
    note2 = swap(note, "zl")
    first = (
        lax.all_to_all(jnp.broadcast_to(source_cells[None], (4, TILE, D)), "zh", 0, 0),
        note2,
        swap(note2, "core"),
        swap(note, "core"),
        swap(target_cells, "core"),
        source_logmass.astype(F32).reshape(1, TILE),
        target_cells,
    )
    column_cells, note2, note3, note1, t1, own_mass, t0 = lax.optimization_barrier(first)
    t2 = swap(t0, "zl")
    notes = (note, note1, note2, note3)
    targets = (target_cells, t1, t2, swap(t2, "core"))
    cells = lax.all_to_all(jnp.broadcast_to(column_cells[None], (4, 4, TILE, D)), "x", 0, 0)
    cells = cells.reshape(NA * TILE, D)

    rows_to = (VM, SHAPE((16, NA, TILE), F32))
    cols_to = (VM, SHAPE((16, NB, TILE), F32))
    rows_state = (VM, SHAPE((NA, TILE), F32))
    cols_state = (VM, SHAPE((NB, TILE), F32))
    tiles = (HERE, SHAPE((SLOTS, TILE, TILE), F32))
    row_blocks = pltpu.VMEM((NA, TILE, TILE), F32)
    col_rows = pltpu.VMEM((NB, 8, TILE), F32)
    gathered = pltpu.VMEM((4, TB_DEV * TILE, D), jnp.bfloat16)
    gathered_sems = pltpu.SemaphoreType.DMA((5,))
    gathered_refs = [(VM, cells), (FAR, targets[0]), *[(ANY, value) for value in targets[1:]]]

    (tile_list,) = call(
        plan_kernel,
        "plan",
        [(SM, note) for note in notes],
        [(KEPT, SHAPE((SLOTS + 8,), jnp.int32))],
        [],
        moved=10 << 20,
    )
    send, x, k = call(
        scores_kernel,
        "scores",
        [
            (KEPT, tile_list), *gathered_refs,
            (FAR, mapping), (VM, own_mass),
        ],
        [(VM, SHAPE((16, NA + 8, TILE), F32)), tiles, tiles],
        [
            gathered, pltpu.VMEM((D, D), jnp.bfloat16), pltpu.VMEM((NA * TILE, D), jnp.bfloat16),
            row_blocks, row_blocks, gathered_sems,
        ],
    )
    tile_list, x = (KEPT, tile_list), (HERE, x)
    recv = row_exchange(send)
    send, u, source_mass = call(
        first_targets_kernel,
        "first_targets",
        [tile_list, (VM, recv), x, (HERE, k)],
        [cols_to, rows_state, rows_state],
        [row_blocks, col_rows, col_rows],
    )
    recv = col_exchange(send)
    send, v, target_mass, k = call(
        kernel_matrix_kernel,
        "kernel_matrix",
        [tile_list, (VM, recv), (VM, u), *[(VM, note) for note in notes], x, (HERE, k)],
        [rows_to, cols_state, cols_state, tiles],
        [row_blocks, row_blocks],
        aliases={8: 3},
    )
    k = (HERE, k)
    for sweep in range(1, SINK):
        recv = row_exchange(send)
        send, *kept = call(
            columns_kernel,
            "columns",
            [tile_list, (VM, recv), (VM, source_mass), k, x],
            [cols_to, *([rows_state] if sweep == SINK - 1 else [])],
            [row_blocks, col_rows],
        )
        recv = col_exchange(send)
        if sweep < SINK - 1:
            (send,) = call(
                rows_kernel,
                "rows",
                [tile_list, (VM, recv), (VM, target_mass), k, x],
                [rows_to],
                [pltpu.VMEM((NB, TILE), F32), row_blocks],
            )
    (alpha,) = kept
    send, beta, column_sum, row_cost = call(
        masses_kernel,
        "masses",
        [tile_list, (VM, recv), (VM, target_mass), k, x],
        [(VM, SHAPE((16, 2 * NA, TILE), F32)), cols_state, cols_state, rows_state],
        [row_blocks, row_blocks],
    )
    recv = row_exchange(send)
    send, row_sum, column_cost = call(
        first_ratio_kernel,
        "first_ratio",
        [tile_list, (VM, recv), (VM, alpha), k, x],
        [cols_to, rows_state, cols_state],
        [row_blocks, row_blocks, col_rows, col_rows],
    )
    recv = col_exchange(send)
    for step in range(1, ADJ):
        (send,) = call(
            pull_kernel,
            "pull",
            [tile_list, (VM, recv), (VM, column_sum), (VM, beta), (VM, row_cost), k, x],
            [rows_to],
            [row_blocks, pltpu.VMEM((NB, TILE), F32)],
        )
        recv = row_exchange(send)
        send, *kept = call(
            push_kernel,
            "push",
            [tile_list, (VM, recv), (VM, row_sum), (VM, alpha), (VM, column_cost), k, x],
            [cols_to, *([rows_state] if step == ADJ - 1 else [])],
            [row_blocks, col_rows],
        )
        recv = col_exchange(send)
    (s,) = kept
    gradient, own_source, own_target = call(
        gradient_kernel,
        "gradient",
        [
            tile_list, (VM, recv), (VM, column_sum), (VM, beta), (VM, alpha), (VM, s), (VM, u), (VM, v),
            *gathered_refs, x,
        ],
        [(VM, SHAPE((D, D), F32)), (VM, SHAPE((1, TILE), F32)), (VM, SHAPE((TB_DEV, TILE), F32))],
        [
            gathered, row_blocks, row_blocks, pltpu.VMEM((NB, TILE), F32), pltpu.VMEM((NB, TILE), F32),
            pltpu.VMEM((NA * TILE, D), F32),
            pltpu.VMEM((CHUNK, TILE, TILE), jnp.bfloat16), pltpu.VMEM((CHUNK, TILE, D), F32), gathered_sems,
        ],
    )
    piece = jnp.sum(col_exchange(gradient.reshape(16, 16, D)), axis=0)
    piece = jnp.sum(row_exchange(jnp.broadcast_to(piece[None], (16, 16, D))), axis=0)
    map_gradient = col_exchange(jnp.broadcast_to(piece[None], (16, 16, D))).reshape(D, D)

    return (own_source.reshape(TILE), own_target.reshape(TB_DEV * TILE), map_gradient)


def solution(mesh):
    grid = Mesh(mesh.devices.reshape(4, 4, 4, 2, 2), AXES)
    tgt = ("x", "zh", "zl", "core")
    both = ("src", *tgt)
    in_specs = (
        P(both, None),
        P(tgt, None),
        P(),
        P(both),
        P(tgt),
        P(),
        P(both, None),
        P(both, None),
    )
    out_specs = (P(both), P(tgt), P())
    return jax.shard_map(shards, mesh=grid, in_specs=in_specs, out_specs=out_specs, check_vma=False)
```
